256 devices in a mesh: orb: 32 (over y, z), row: 8 (over x, core).
Axes of the slice: x: 4, y: 4, z: 8, core: 2. Of those that a mesh axis runs over, the one named last changes fastest.
Arguments:
- orbital_fragments: bfloat16 [1572864, 128], P(('orb', 'row')), may hold values from -6 to 6
- receiving_devices: int32 [1572864, 1], P(('orb', 'row')), may hold values from 0 to 255; in each aligned block of 6144 rows (0 to 6143, 6144 to 12287, ...) at most 48 rows name the same one
- fragment_grid_tile: int32 [1572864], P(('orb', 'row')), may hold values from 0 to 767
- outside_field_grid: float32 [196608, 128], P(('orb', 'row')), may hold values from -6 to 6
- density_matrix_tiles: bfloat16 [512, 12, 128, 128], P(('orb', 'row')), may hold values from -2 to 2
- energy_operator_tiles: bfloat16 [512, 12, 128, 128], P(('orb', 'row')), may hold values from -0.796875 to 0.796875
- tile_column_numbers: int32 [512, 12], P('orb'), may hold values from 0 to 511, as said below
Outputs:
- applied: bfloat16 [1572864, 128], P(('orb', 'row'))
- charge_distribution: float32 [196608, 128], P(('orb', 'row'))
- product: bfloat16 [512, 12, 128, 128], P(('orb', 'row'))
The draws below stay inside these ranges and needn't reach their ends.
Inputs may be any that keep to these rules, and one draw needn't show every extreme that they name: `receiving_devices`: among the 6144 segments of one device at most 48 have the same target, and some target has exactly 48. `tile_column_numbers`: block row i names 12 distinct block columns j with j // 16 == i // 16; its first is i itself.
All inputs are finite; a program needn't handle non-finite values.
Results may differ from the reference program's by a relative error of at most 0.0044.
Values may be sent and summed in bfloat16 or wider, within the bound.
No kernel may reach another device: no remote copies, remote signals or barrier semaphores. Data moves between devices by JAX's collectives and lax.ppermute only.
A program may use at most 64 MiB of HBM per device.

```python
import math
import jax
import jax.numpy as jnp
import numpy as np
from jax import lax

BLK = 128
SEGL = 128
SEGF = 24
NNZ = 12
SEG_DEV = 6144
SEGS = 1572864
CAP = 48
RB = 768
CELLS = 196608
NB = 512
G = 16
DEVICES = 256


def draw_tile_column_numbers(key, part):
    keys = jax.random.split(jax.random.fold_in(key, 17), NB)

    def offsets_of(row_random_key):
        return jax.random.permutation(row_random_key, G - 1)[:NNZ - 1] + 1
    offsets = jax.vmap(offsets_of)(keys).astype(jnp.int32)
    offsets = jnp.concatenate([jnp.zeros((NB, 1), jnp.int32), offsets], axis=1)
    rows = jnp.arange(NB, dtype=jnp.int32)
    local = rows % G
    return (rows - local)[:, None] + (local[:, None] + offsets) % G


def draw_outside_field_grid(key, part):
    key_offset, noise_random_key = jax.random.split(jax.random.fold_in(key, 29))
    start_offset = jax.random.uniform(key_offset, (CELLS, 1), jnp.float32, -4.0, 4.0)
    noise = jnp.clip(jax.random.normal(noise_random_key, (CELLS, SEGL), jnp.float32), -2.0, 2.0)
    return start_offset + noise


def touch_ends(result, rng, least, largest):
    shape = result.shape
    place = [jax.random.randint(jax.random.fold_in(rng, axis), (), 0, shape[axis]) for axis in range(len(shape))]
    result = result.at[tuple(place)].set(least)
    longest = shape.index(max(shape))
    place[longest] = (place[longest] + 1) % shape[longest]
    return result.at[tuple(place)].set(largest)


def steps_of(key, dims, cuts, low, top_value):
    level = 1.0
    for axis_at, blocks in cuts:
        draws = jax.random.uniform(jax.random.fold_in(jax.random.fold_in(key, 6), axis_at), (blocks,), jnp.float32, low / len(cuts), top_value / len(cuts))
        level = level * jnp.repeat(jnp.exp(draws), dims[axis_at] // blocks).reshape((-1,) + (1,) * (len(dims) - 1 - axis_at))
    return level


def assign_block(stream_key, own, number, rows, count, top, limit, skew):
    sequence = jax.random.permutation(stream_key, count)
    heavy_load, ordinary = shares(count, rows * top, limit, skew, True), shares(count, rows * top, limit, skew, False)
    places = jnp.arange(count)

    def named(sizes, rotation):
        used = int((sizes > 0).sum())
        fixed = max(1, used // 4)
        shifted = fixed + (places - fixed + rotation * (used - fixed)) % max(1, count - fixed)
        return jnp.zeros((count,), jnp.int32).at[sequence[jnp.where(places < fixed, places, shifted)]].set(jnp.asarray(sizes, jnp.int32))

    sizes = jnp.where(number % 4 == 0, named(heavy_load, number // 4), named(ordinary, number - number // 4 - 1))
    mixed = jax.random.permutation(jax.random.fold_in(own, 3), count)
    donor, taker = mixed[0:count // 2 * 2:2], mixed[1:count // 2 * 2:2]
    room = jnp.minimum(sizes[donor] - 1, limit - sizes[taker]) // 2
    room = jnp.where((donor == sequence[0]) | (taker == sequence[0]) | (sizes[taker] == 0), 0, jnp.maximum(room, 0))
    shifted = jax.random.randint(jax.random.fold_in(own, 4), (count // 2,), 0, 1 << 20) % (room + 1)
    sizes = sizes.at[donor].add(-shifted).at[taker].add(shifted)
    labels = jnp.searchsorted(jnp.cumsum(sizes), jnp.arange(rows * top), side="right").astype(jnp.int32)
    grid = labels.reshape(top, rows).T
    grid = grid[jax.random.permutation(jax.random.fold_in(own, 1), rows)]
    rotation = jax.random.randint(jax.random.fold_in(own, 2), (rows, 1), 0, top)
    return jnp.take_along_axis(grid, (jnp.arange(top)[None, :] + rotation) % top, axis=1)


def shares(count, total, most, slope, full):
    weights = [(1 << 20) // math.isqrt(standing ** slope) + 1 for standing in range(1, count + 1)]
    largest = most if full else min(most, max(-(-total // count), total * weights[0] // sum(weights)))
    least = 1 if total - largest >= count - 1 else 0
    counts, surplus = [largest] + [least] * (count - 1), total - largest - least * (count - 1)
    while surplus > 0:
        candidates = [i for i in range(1, count) if counts[i] < largest] or [i for i in range(1, count) if counts[i] < most]
        mass, remaining = sum([weights[i] for i in candidates]), surplus
        for i in candidates:
            addition = min(most - counts[i], max(1, remaining * weights[i] // mass), surplus)
            counts[i] = counts[i] + addition
            surplus = surplus - addition
    return np.array(counts)


def bell_draw(stream_key, shape, width, limit, pieces=(), kind=jnp.bfloat16):
    array = jax.random.normal(stream_key, shape, jnp.float32) * width
    if len(pieces) > 0:
        array = steps_of(stream_key, shape, pieces, -0.22, 0.18) * array
    return jnp.clip(array, min=-limit, max=limit).astype(kind)


def setup_inputs(seed: int = 0) -> dict:
    key_list = jax.random.split(jax.random.key(seed), 8)
    orbital_fragments = bell_draw(key_list[0], (SEGS, SEGL), 1.0, 6.0, ((0, 256),))
    receiving_devices_keys = jax.random.split(jax.random.fold_in(key_list[1], 1), SEGS // SEG_DEV)
    receiving_devices_turns = jax.random.permutation(jax.random.fold_in(key_list[1], 3), SEGS // SEG_DEV)
    receiving_devices = jax.vmap(lambda own, number: assign_block(jax.random.fold_in(key_list[1], 2), own, number, SEG_DEV, DEVICES, 1, CAP, 2))(receiving_devices_keys, receiving_devices_turns).reshape((SEGS, 1))
    fragment_grid_tile = touch_ends(jax.random.randint(key_list[2], (SEGS,), 0, RB), jax.random.fold_in(key_list[2], 1), 0, RB - 1).astype(jnp.int32)
    outside_field_grid = draw_outside_field_grid(jax.random.fold_in(key_list[7], 71), 0)
    density_matrix_tiles = bell_draw(key_list[4], (NB, NNZ, BLK, BLK), 0.25, 2.0, ((0, 256),))
    energy_operator_tiles = bell_draw(key_list[5], (NB, NNZ, BLK, BLK), 0.1, 0.796875, ((0, 256),))
    tile_column_numbers = draw_tile_column_numbers(jax.random.fold_in(key_list[7], 71), 0)
    return dict(orbital_fragments=orbital_fragments, receiving_devices=receiving_devices, fragment_grid_tile=fragment_grid_tile, outside_field_grid=outside_field_grid, density_matrix_tiles=density_matrix_tiles, energy_operator_tiles=energy_operator_tiles, tile_column_numbers=tile_column_numbers)


def reference(orbital_fragments, receiving_devices, fragment_grid_tile, outside_field_grid, density_matrix_tiles, energy_operator_tiles, tile_column_numbers):
    dest = (receiving_devices[:, 0] * RB + fragment_grid_tile).astype(jnp.int32)
    values = orbital_fragments.astype(jnp.float32)
    charge_distribution = jax.ops.segment_sum(values * values, dest, num_segments=RB * DEVICES)
    effective_field_values = outside_field_grid - 1.5 * jnp.cbrt(1.0 + charge_distribution)
    applied = (effective_field_values[dest] * values).astype(jnp.bfloat16)
    weighted = (values * applied.astype(jnp.float32)).reshape(-1, SEGF * SEGL)
    shift = (jnp.sum(weighted, axis=1) / (SEGF * SEGL)).astype(jnp.bfloat16)
    shift_rows = shift.reshape(-1, BLK)

    def one_row(index):
        columns = tile_column_numbers[index]
        rows_h = energy_operator_tiles[columns].astype(jnp.float32)
        row_sparsity_pattern = tile_column_numbers[columns]
        match = (row_sparsity_pattern[:, :, None] == columns[None, None, :]).astype(jnp.float32)
        selected = jnp.einsum('efg,efab->egab', match, rows_h)
        kernel_row = density_matrix_tiles[index].astype(jnp.float32)
        main = jnp.einsum('eab,egbc->gac', kernel_row, selected)
        diag = kernel_row * shift_rows[columns].astype(jnp.float32)[:, None, :]
        return (main + diag).astype(jnp.bfloat16)

    product = lax.map(one_row, jnp.arange(NB, dtype=jnp.int32))
    return applied, charge_distribution, product
```

```python
import functools

import jax
import jax.numpy as jnp
from jax import lax
from jax.experimental import pallas as pl
from jax.experimental.pallas import tpu as pltpu
from jax.sharding import PartitionSpec as P

BLK = 128
SEGF = 24
CAP = 48
LANES = 128
F32 = jnp.float32
BF16 = jnp.bfloat16
VMEM = pl.BlockSpec(memory_space=pltpu.VMEM)
SMEM = pl.BlockSpec(memory_space=pltpu.SMEM)


def params(mib):
    return pltpu.CompilerParams(vmem_limit_bytes=mib << 20)


def cost(us, nbytes):
    return pl.CostEstimate(
        flops=int(us * 1e9), bytes_accessed=int(nbytes), transcendentals=0
    )


def iota(shape, axis):
    return lax.broadcasted_iota(jnp.int32, shape, axis)


def rank_kernel(devices, dest_ref, tile_ref, slot_ref, label_ref, run, acc):
    blocks = dest_ref.shape[0]
    owner = iota((devices, LANES), 0)
    src, dst = iota((LANES, 2 * LANES), 0), iota((LANES, 2 * LANES), 1)
    tri = ((dst >= LANES) | (src < dst)).astype(F32).astype(BF16)
    place = iota((LANES, LANES), 0)
    run[...] = jnp.zeros_like(run)
    acc[...] = jnp.zeros_like(acc)

    def step(b, carry):
        d = dest_ref[pl.ds(b, 1), :]
        hit = owner == d
        hot = hit.astype(F32).astype(BF16)
        counts = jnp.dot(hot, tri, preferred_element_type=F32)
        before = counts[:, :LANES] + run[...]
        rank = jnp.sum(jnp.where(hit, before, 0.0), axis=0, keepdims=True)
        run[...] += counts[:, LANES:]
        rank = rank.astype(jnp.int32)
        slot_ref[pl.ds(b, 1), :] = d * CAP + rank
        label = tile_ref[pl.ds(b, 1), :] + 1
        high = (label >> 2).astype(F32)
        low = (label & 3).astype(F32)
        spread = jnp.where(place == rank, high, 0.0)
        spread = spread + jnp.where(place == rank + 64, low, 0.0)
        acc[...] += lax.dot_general(
            hot,
            spread.astype(BF16),
            (((1,), (1,)), ((), ())),
            preferred_element_type=F32,
        )
        return carry

    lax.fori_loop(0, blocks, step, 0, unroll=4)
    both = acc[...]
    label_ref[...] = (both * 4.0 + pltpu.roll(both, 64, 1)).astype(jnp.int32) - 1


def rank_and_labels(dest, tile, devices):
    blocks = dest.shape[0]
    return pl.pallas_call(
        functools.partial(rank_kernel, devices),
        out_shape=(
            jax.ShapeDtypeStruct((blocks, LANES), jnp.int32),
            jax.ShapeDtypeStruct((devices, LANES), jnp.int32),
        ),
        in_specs=[VMEM, VMEM],
        out_specs=(VMEM, VMEM),
        scratch_shapes=[
            pltpu.VMEM((devices, LANES), F32),
            pltpu.VMEM((devices, LANES), F32),
        ],
        compiler_params=params(4),
        cost_estimate=cost(5, 1 << 18),
        name="rank",
    )(dest, tile)


def pack_kernel(slot_ref, x_ref, out_ref, xf, of):
    rows = x_ref.shape[0]
    slots = out_ref.shape[0]

    def widen(i, c):
        at = pl.ds(pl.multiple_of(i * 256, 256), 256)
        xf[at, :] = x_ref[at, :].astype(F32)
        return c

    lax.fori_loop(0, rows // 256, widen, 0)

    def clear(i, c):
        of[pl.ds(pl.multiple_of(i * 512, 512), 512), :] = jnp.zeros((512, LANES), F32)
        return c

    lax.fori_loop(0, slots // 512, clear, 0)

    def move(i, c):
        b = i // 4
        first = (i % 4) * 32
        for j in range(32):
            s = slot_ref[b, first + j]
            of[pl.ds(s, 1), :] = xf[pl.ds(i * 32 + j, 1), :]
        return c

    lax.fori_loop(0, rows // 32, move, 0)

    def narrow(i, c):
        at = pl.ds(pl.multiple_of(i * 256, 256), 256)
        out_ref[at, :] = of[at, :].astype(BF16)
        return c

    lax.fori_loop(0, slots // 256, narrow, 0)


def pack(slot, x, slots):
    rows = x.shape[0]
    return pl.pallas_call(
        pack_kernel,
        out_shape=jax.ShapeDtypeStruct((slots, LANES), BF16),
        in_specs=[SMEM, VMEM],
        out_specs=VMEM,
        scratch_shapes=[pltpu.VMEM((rows, LANES), F32), pltpu.VMEM((slots, LANES), F32)],
        compiler_params=params(17),
        cost_estimate=cost(12, 5 << 20),
        name="pack",
    )(slot, x)


def owner_kernel(label_ref, v_ref, field_ref, out_ref, charge_ref, acc, pot):
    slots = v_ref.shape[0]
    tiles = field_ref.shape[0]
    acc[...] = jnp.zeros_like(acc)
    depth = 512
    cell = iota((tiles, LANES), 0)

    def add(k, c):
        hot = []
        for j in range(depth // LANES):
            lab = label_ref[pl.ds(k * (depth // LANES) + j, 1), :]
            hot.append((cell == lab).astype(F32).astype(BF16))
        v = v_ref[pl.ds(pl.multiple_of(k * depth, depth), depth), :].astype(F32)
        square = v * v
        high = square.astype(BF16)
        low = (square - high.astype(F32)).astype(BF16)
        acc[...] += jnp.dot(
            jnp.concatenate(hot, axis=1),
            jnp.concatenate([high, low], axis=1),
            preferred_element_type=F32,
        )
        return c

    lax.fori_loop(0, slots // depth, add, 0)
    charge = acc[:, :LANES] + acc[:, LANES:]
    charge_ref[...] = charge
    field = field_ref[...] - 1.5 * jnp.exp(jnp.log(1.0 + charge) * (1.0 / 3.0))
    high = field.astype(BF16)
    pot[:, :LANES] = high
    pot[:, LANES:] = (field - high.astype(F32)).astype(BF16)
    chunk = 512
    lane = iota((LANES, tiles), 1)

    def apply(k, c):
        hot = []
        for j in range(chunk // LANES):
            lab = label_ref[pl.ds(k * (chunk // LANES) + j, 1), :]
            col = jnp.transpose(jnp.broadcast_to(lab, (LANES, LANES)))
            wide = jnp.concatenate([col] * (tiles // LANES), axis=1)
            hot.append((lane == wide).astype(F32).astype(BF16))
        got = jnp.dot(jnp.concatenate(hot, axis=0), pot[...], preferred_element_type=F32)
        at = pl.ds(pl.multiple_of(k * chunk, chunk), chunk)
        here = got[:, :LANES] + got[:, LANES:]
        out_ref[at, :] = (here * v_ref[at, :].astype(F32)).astype(BF16)
        return c

    lax.fori_loop(0, slots // chunk, apply, 0)


def owner_step(label, values, field):
    slots = values.shape[0]
    tiles = field.shape[0]
    return pl.pallas_call(
        owner_kernel,
        out_shape=(
            jax.ShapeDtypeStruct((slots, LANES), BF16),
            jax.ShapeDtypeStruct((tiles, LANES), F32),
        ),
        in_specs=[VMEM, VMEM, VMEM],
        out_specs=(VMEM, VMEM),
        scratch_shapes=[
            pltpu.VMEM((tiles, 2 * LANES), F32),
            pltpu.VMEM((tiles, 2 * LANES), BF16),
        ],
        compiler_params=params(18),
        cost_estimate=cost(20, 7 << 20),
        name="owner",
    )(label, values, field)


def unpack_kernel(n_row, slot_ref, ret_ref, x_ref, out_ref, shift_ref, rf, of, part):
    rows = x_ref.shape[0]
    slots = ret_ref.shape[0]

    def widen(i, c):
        at = pl.ds(pl.multiple_of(i * 256, 256), 256)
        rf[at, :] = ret_ref[at, :].astype(F32)
        return c

    lax.fori_loop(0, slots // 256, widen, 0)

    def move(i, c):
        b = i // 4
        first = (i % 4) * 32
        for j in range(32):
            s = slot_ref[b, first + j]
            of[pl.ds(i * 32 + j, 1), :] = rf[pl.ds(s, 1), :]
        return c

    lax.fori_loop(0, rows // 32, move, 0)
    count = 8

    def finish(i, c):
        at = pl.ds(pl.multiple_of(i * count * SEGF, count * SEGF), count * SEGF)
        got = of[at, :]
        out_ref[at, :] = got.astype(BF16)
        work = (got * x_ref[at, :].astype(F32)).reshape(count, SEGF, LANES)
        part[pl.ds(pl.multiple_of(i * count, count), count), :] = jnp.sum(work, axis=1)
        return c

    lax.fori_loop(0, rows // (count * SEGF), finish, 0)
    functions = rows // SEGF
    total = lax.dot_general(
        jnp.ones((8, LANES), F32),
        part[...],
        (((1,), (1,)), ((), ())),
        precision=lax.Precision.HIGHEST,
        preferred_element_type=F32,
    )
    total = total * (1.0 / (SEGF * LANES))
    one = jnp.concatenate(
        [total[0:1, i * BLK : (i + 1) * BLK] for i in range(functions // BLK)]
        + [jnp.zeros((8 - functions // BLK, BLK), F32)],
        axis=0,
    )
    one = one.astype(BF16).astype(F32)
    for r in range(n_row):
        shift_ref[r] = one


def unpack(slot, ret, x, n_row):
    rows = x.shape[0]
    slots = ret.shape[0]
    return pl.pallas_call(
        functools.partial(unpack_kernel, n_row),
        out_shape=(
            jax.ShapeDtypeStruct((rows, LANES), BF16),
            jax.ShapeDtypeStruct((n_row, 8, LANES), F32),
        ),
        in_specs=[SMEM, VMEM, VMEM],
        out_specs=(VMEM, VMEM),
        scratch_shapes=[
            pltpu.VMEM((slots, LANES), F32),
            pltpu.VMEM((rows, LANES), F32),
            pltpu.VMEM((rows // SEGF, LANES), F32),
        ],
        compiler_params=params(19),
        cost_estimate=cost(12, 7 << 20),
        name="unpack",
    )(slot, ret, x)


def main_kernel(row_at, col_at, d_ref, *refs):
    bufs, (out_ref, sel, dcat) = refs[:-3], refs[-3:]
    rows, nnz = d_ref.shape[:2]
    width = nnz * BLK

    def one(i, carry):
        def clear(e, c):
            sel[pl.ds(pl.multiple_of(e * BLK, BLK), BLK), :] = jnp.zeros(
                (BLK, sel.shape[1]), BF16
            )
            return c

        lax.fori_loop(0, nnz, clear, 0)
        for e in range(nnz):
            dcat[:, e * BLK : (e + 1) * BLK] = d_ref[i, e]
        for b, buf in enumerate(bufs):
            for j in range(rows):
                e = row_at[i, b * rows + j]

                @pl.when(e < nnz)
                def _():
                    top = pl.multiple_of(e * BLK, BLK)

                    def put(f, c):
                        g = col_at[i, (b * rows + j) * nnz + f]
                        left = pl.multiple_of(g * BLK, BLK)
                        sel[pl.ds(top, BLK), pl.ds(left, BLK)] = buf[j, f]
                        return c

                    lax.fori_loop(0, nnz, put, 0)

        def mult(n, c):
            at = pl.ds(pl.multiple_of(n * 256, 256), 256)
            out_ref[i, :, at] = jnp.dot(dcat[...], sel[:, at], preferred_element_type=F32)
            return c

        lax.fori_loop(0, width // 256, mult, 0)
        return carry

    lax.fori_loop(0, rows, one, 0)


def main_product(row_at, col_at, d, bufs):
    rows, nnz = d.shape[:2]
    return pl.pallas_call(
        main_kernel,
        out_shape=jax.ShapeDtypeStruct((rows, BLK, nnz * BLK), F32),
        in_specs=[SMEM, SMEM, VMEM] + [VMEM] * len(bufs),
        out_specs=VMEM,
        scratch_shapes=[
            pltpu.VMEM((nnz * BLK, (nnz + 1) * BLK), BF16),
            pltpu.VMEM((BLK, nnz * BLK), BF16),
        ],
        compiler_params=params(18),
        cost_estimate=cost(10, 10 << 20),
        name="hamiltonian",
    )(row_at, col_at, d, *bufs)


def final_kernel(at_ref, main_ref, d_ref, shift_ref, out_ref):
    rows, nnz = d_ref.shape[:2]
    for i in range(rows):
        for g in range(nnz):
            s = shift_ref[pl.ds(at_ref[i, g], 1), :]
            out_ref[i, g] = (
                main_ref[i, :, g * BLK : (g + 1) * BLK] + d_ref[i, g].astype(F32) * s
            ).astype(BF16)


def final(at, main, d, shift):
    return pl.pallas_call(
        final_kernel,
        out_shape=jax.ShapeDtypeStruct(d.shape, BF16),
        in_specs=[SMEM, VMEM, VMEM, VMEM],
        out_specs=VMEM,
        compiler_params=params(6),
        cost_estimate=cost(2, 4 << 20),
        name="final",
    )(at, main, d, shift)


def gather_hamiltonian(tiles, n_row):
    chips = n_row // 2
    same = [tiles]
    for d in range(1, chips):
        perm = [(r, ((r // 2 + d) % chips) * 2 + r % 2) for r in range(n_row)]
        same.append(lax.ppermute(tiles, "row", perm))
    swap = [(r, r ^ 1) for r in range(n_row)]
    other = [lax.ppermute(t, "row", swap) for t in same]
    return same + other


def positions(pattern, own_rows, n_row):
    me = lax.axis_index("row")
    chips = n_row // 2
    chip, core = me // 2, me % 2
    back = jnp.arange(chips, dtype=jnp.int32)
    owner = (chip - back + chips) % chips * 2
    owner = jnp.concatenate([owner + core, owner + 1 - core])
    k = (owner[:, None] * own_rows + jnp.arange(own_rows, dtype=jnp.int32)).reshape(-1)
    own = lax.dynamic_slice_in_dim(pattern, me * own_rows, own_rows, 0)
    nnz = pattern.shape[1]
    local = own % (own_rows * n_row)
    index = jnp.arange(nnz, dtype=jnp.int32)
    row_at = jnp.min(
        jnp.where(local[:, None, :] == k[None, :, None], index, nnz), axis=2
    )
    rows = pattern[k]
    col_at = jnp.min(
        jnp.where(own[:, None, None, :] == rows[None, :, :, None], index, nnz), axis=3
    )
    shift_at = local // own_rows * 8 + local % own_rows
    return row_at, col_at.reshape(own_rows, -1), shift_at


def body(
    orbital_fragments,
    receiving_devices,
    fragment_grid_tile,
    outside_field_grid,
    density_matrix_tiles,
    energy_operator_tiles,
    tile_column_numbers,
):
    seg_dev = orbital_fragments.shape[0]
    n_orb = lax.axis_size("orb")
    n_row = lax.axis_size("row")
    devices = n_orb * n_row
    slots = devices * CAP
    axes = ("orb", "row")

    def exchange(x):
        return lax.all_to_all(x, axes, split_axis=0, concat_axis=0, tiled=True)

    dest = receiving_devices.reshape(seg_dev // LANES, LANES)
    tile = fragment_grid_tile.reshape(seg_dev // LANES, LANES)
    slot, labels = rank_and_labels(dest, tile, devices)
    labels = exchange(labels.reshape(devices, 1, LANES)).reshape(devices, LANES)
    where = labels[:, :CAP].reshape(slots // LANES, LANES)
    outgoing = pack(slot, orbital_fragments, slots)
    arrived = exchange(outgoing.reshape(devices, CAP, LANES)).reshape(slots, LANES)

    own_rows = density_matrix_tiles.shape[0]
    row_at, col_at, shift_at = positions(tile_column_numbers, own_rows, n_row)
    bufs = gather_hamiltonian(energy_operator_tiles, n_row)
    main = main_product(row_at, col_at, density_matrix_tiles, bufs)

    arrived, main = lax.optimization_barrier((arrived, main))
    results, charge = owner_step(where, arrived, outside_field_grid)
    returned = exchange(results.reshape(devices, CAP, LANES)).reshape(slots, LANES)
    applied, shift = unpack(slot, returned, orbital_fragments, n_row)
    shift = lax.all_to_all(shift, "row", split_axis=0, concat_axis=0, tiled=True)
    product = final(shift_at, main, density_matrix_tiles, shift.reshape(n_row * 8, LANES))
    return (applied, charge, product)


def solution(mesh):
    return jax.shard_map(
        body,
        mesh=mesh,
        in_specs=(
            P(("orb", "row"), None),
            P(("orb", "row"), None),
            P(("orb", "row")),
            P(("orb", "row"), None),
            P(("orb", "row"), None, None, None),
            P(("orb", "row"), None, None, None),
            P("orb", None),
        ),
        out_specs=(
            P(("orb", "row"), None),
            P(("orb", "row"), None),
            P(("orb", "row"), None, None, None),
        ),
        check_vma=False,
    )
```

```python
import functools

import jax
import jax.numpy as jnp
from jax import lax
from jax.experimental import pallas as pl
from jax.experimental.pallas import tpu as pltpu
from jax.sharding import PartitionSpec as P

BLK = 128
SEGF = 24
CAP = 48
PAIR = 50
LANES = 128
F32 = jnp.float32
BF16 = jnp.bfloat16
VMEM = pl.BlockSpec(memory_space=pltpu.VMEM)
SMEM = pl.BlockSpec(memory_space=pltpu.SMEM)


def params(mib):
    return pltpu.CompilerParams(vmem_limit_bytes=mib << 20)


def cost(us, nbytes):
    return pl.CostEstimate(
        flops=int(us * 1e9), bytes_accessed=int(nbytes), transcendentals=0
    )


def iota(shape, axis):
    return lax.broadcasted_iota(jnp.int32, shape, axis)


def hot_rows(wide, which):
    return (wide == which).astype(F32).astype(BF16)


def columns(row):
    return jnp.transpose(jnp.broadcast_to(row, (LANES, LANES)))


def rank_kernel(devices, me_ref, dest_ref, tile_ref, slot_ref, high_ref, low_ref, acc):
    blocks = dest_ref.shape[0]
    owner = iota((LANES, devices), 1)
    dst, src = iota((LANES + 8, LANES), 0), iota((LANES + 8, LANES), 1)
    tri = ((dst >= LANES) | (src < dst)).astype(F32).astype(BF16)
    ones = jnp.ones((8, devices), BF16)
    place = iota((LANES, LANES), 0)
    turn = (me_ref[0] * PAIR) & (LANES - 1)
    acc[...] = jnp.zeros_like(acc)
    group = 4

    def step(q, run):
        hots, spreads = [], []
        for j in range(group):
            b = q * group + j
            d = dest_ref[pl.ds(b, 1), :]
            wide = jnp.concatenate([columns(d)] * (devices // LANES), axis=1)
            hit = owner == wide
            hot = hit.astype(F32).astype(BF16)
            hots.append(hot)
            counts = jnp.dot(tri, hot, preferred_element_type=F32)
            before = counts[:LANES] + run[0:1]
            run = run + counts[LANES:]
            mine = jnp.where(hit, before, 0.0).astype(BF16)
            rank = lax.dot_general(
                ones, mine, (((1,), (1,)), ((), ())), preferred_element_type=F32
            )
            rank = rank[0:1].astype(jnp.int32)
            slot_ref[pl.ds(b, 1), :] = d * PAIR + rank
            label = tile_ref[pl.ds(b, 1), :] + 1
            at = place == ((rank + turn) & (LANES - 1))
            high = jnp.where(at, (label >> 2).astype(F32), 0.0)
            low = jnp.where(at, (label & 3).astype(F32), 0.0)
            spreads.append(jnp.concatenate([high, low], axis=0).astype(BF16))
        acc[...] += jnp.dot(
            jnp.concatenate(spreads, axis=1),
            jnp.concatenate(hots, axis=0),
            preferred_element_type=F32,
        )
        return run

    lax.fori_loop(0, blocks // group, step, jnp.zeros((8, devices), F32))
    high_ref[...] = jnp.transpose(acc[:LANES, :])
    low_ref[...] = jnp.transpose(acc[LANES:, :])


def ranks(me, dest, tile, devices):
    blocks = dest.shape[0]
    return pl.pallas_call(
        functools.partial(rank_kernel, devices),
        out_shape=(
            jax.ShapeDtypeStruct((blocks, LANES), jnp.int32),
            jax.ShapeDtypeStruct((devices, LANES), F32),
            jax.ShapeDtypeStruct((devices, LANES), F32),
        ),
        in_specs=[SMEM, VMEM, VMEM],
        out_specs=(VMEM,) * 3,
        scratch_shapes=[pltpu.VMEM((2 * LANES, devices), F32)],
        compiler_params=params(5),
        cost_estimate=cost(4, 1 << 18),
        name="rank",
    )(me, dest, tile)


ROWS = 64


def widen(src_ref, dst):
    def step(i, c):
        at = pl.ds(pl.multiple_of(i * 256, 256), 256)
        dst[at, :] = src_ref[at, :].astype(F32)
        return c

    lax.fori_loop(0, src_ref.shape[0] // 256, step, 0)


def pack_kernel(slot_ref, x_ref, high_ref, low_ref, out_ref, xf, of):
    rows = x_ref.shape[0]
    slots = of.shape[0]
    devices = high_ref.shape[0]
    widen(x_ref, xf)

    def clear(i, c):
        of[pl.ds(pl.multiple_of(i * 512, 512), 512), :] = jnp.zeros((512, LANES), F32)
        return c

    lax.fori_loop(0, slots // 512, clear, 0)

    def move(i, c):
        base = i * ROWS
        for j in range(ROWS):
            of[pl.ds(slot_ref[base + j], 1), :] = xf[pl.ds(base + j, 1), :]
        return c

    lax.fori_loop(0, rows // ROWS, move, 0)
    of[pl.ds(CAP, devices, stride=PAIR), :] = high_ref[...]
    of[pl.ds(CAP + 1, devices, stride=PAIR), :] = low_ref[...]

    def narrow(i, c):
        at = pl.ds(pl.multiple_of(i * 256, 256), 256)
        out_ref[at, :] = of[at, :].astype(BF16)
        return c

    lax.fori_loop(0, slots // 256, narrow, 0)


def pack(slot, x, high, low):
    rows = x.shape[0]
    slots = high.shape[0] * PAIR
    return pl.pallas_call(
        pack_kernel,
        out_shape=jax.ShapeDtypeStruct((slots, LANES), BF16),
        in_specs=[SMEM, VMEM, VMEM, VMEM],
        out_specs=VMEM,
        scratch_shapes=[pltpu.VMEM((rows, LANES), F32), pltpu.VMEM((slots, LANES), F32)],
        compiler_params=params(18),
        cost_estimate=cost(10, 5 << 20),
        name="pack",
    )(slot, x, high, low)


DEPTH = 1280
CHUNK = 1280


def slot_labels(high, low):
    devices = high.shape[0]
    groups = -(-devices * PAIR // LANES // 8) * 8
    source, lane = iota((devices, LANES), 0), iota((devices, LANES), 1)
    offset = (source * PAIR) & (LANES - 1)
    near = lane >= offset
    k, s = iota((groups, devices), 0), iota((groups, devices), 1)
    first = (s * PAIR) >> 7
    left = jnp.concatenate([first == k, first + 1 == k], axis=1)
    left = left.astype(F32).astype(BF16)

    def part(x):
        return jnp.concatenate(
            [jnp.where(near, x, 0.0), jnp.where(near, 0.0, x)], axis=0
        ).astype(BF16)

    right = jnp.concatenate([part(high), part(low)], axis=1)
    both = jnp.dot(left, right, preferred_element_type=F32)
    return (both[:, :LANES] * 4.0 + both[:, LANES:]).astype(jnp.int32) - 1


def owner_kernel(v_ref, field_ref, out_ref, charge_ref, vf, label, acc, pot):
    slots = v_ref.shape[0]
    tiles = field_ref.shape[0]
    devices = slots // PAIR
    widen(v_ref, vf)
    label[...] = slot_labels(
        vf[pl.ds(CAP, devices, stride=PAIR), :],
        vf[pl.ds(CAP + 1, devices, stride=PAIR), :],
    )
    acc[...] = jnp.zeros_like(acc)
    cell = iota((tiles, LANES), 0)

    def add(k, c):
        hot = []
        for j in range(DEPTH // LANES):
            hot.append(hot_rows(cell, label[pl.ds(k * (DEPTH // LANES) + j, 1), :]))
        v = vf[pl.ds(pl.multiple_of(k * DEPTH, DEPTH), DEPTH), :]
        square = v * v
        high = square.astype(BF16)
        low = (square - high.astype(F32)).astype(BF16)
        acc[...] += jnp.dot(
            jnp.concatenate(hot, axis=1),
            jnp.concatenate([high, low], axis=1),
            preferred_element_type=F32,
        )
        return c

    lax.fori_loop(0, slots // DEPTH, add, 0)
    charge = acc[:, :LANES] + acc[:, LANES:]
    charge_ref[...] = charge
    field = field_ref[...] - 1.5 * jnp.exp(jnp.log(1.0 + charge) * (1.0 / 3.0))
    high = field.astype(BF16)
    pot[:, :LANES] = high
    pot[:, LANES:] = (field - high.astype(F32)).astype(BF16)
    lane = iota((LANES, tiles), 1)

    def apply(k, c):
        hot = []
        for j in range(CHUNK // LANES):
            col = columns(label[pl.ds(k * (CHUNK // LANES) + j, 1), :])
            hot.append(hot_rows(lane, jnp.concatenate([col] * (tiles // LANES), axis=1)))
        got = jnp.dot(
            jnp.concatenate(hot, axis=0), pot[...], preferred_element_type=F32
        )
        at = pl.ds(pl.multiple_of(k * CHUNK, CHUNK), CHUNK)
        here = got[:, :LANES] + got[:, LANES:]
        out_ref[at, :] = (here * vf[at, :]).astype(BF16)
        return c

    lax.fori_loop(0, slots // CHUNK, apply, 0)


def owner_step(v, field):
    slots = v.shape[0]
    tiles = field.shape[0]
    return pl.pallas_call(
        owner_kernel,
        out_shape=(
            jax.ShapeDtypeStruct(v.shape, BF16),
            jax.ShapeDtypeStruct((tiles, LANES), F32),
        ),
        in_specs=[VMEM] * 2,
        out_specs=(VMEM,) * 2,
        scratch_shapes=[
            pltpu.VMEM((slots, LANES), F32),
            pltpu.VMEM((-(-slots // LANES // 8) * 8, LANES), jnp.int32),
            pltpu.VMEM((tiles, 2 * LANES), F32),
            pltpu.VMEM((tiles, 2 * LANES), BF16),
        ],
        compiler_params=params(28),
        cost_estimate=cost(16, 7 << 20),
        name="owner",
    )(v, field)


def unpack_kernel(n_row, slot_ref, ret_ref, x_ref, out_ref, shift_ref, rf, of, part):
    rows = x_ref.shape[0]
    widen(ret_ref, rf)

    def move(i, c):
        base = i * ROWS
        for j in range(ROWS):
            of[pl.ds(base + j, 1), :] = rf[pl.ds(slot_ref[base + j], 1), :]
        return c

    lax.fori_loop(0, rows // ROWS, move, 0)
    count = 8

    def narrow(i, c):
        at = pl.ds(pl.multiple_of(i * count * SEGF, count * SEGF), count * SEGF)
        got = of[at, :]
        out_ref[at, :] = got.astype(BF16)
        work = (got * x_ref[at, :].astype(F32)).reshape(count, SEGF, LANES)
        part[pl.ds(pl.multiple_of(i * count, count), count), :] = jnp.sum(work, axis=1)
        return c

    lax.fori_loop(0, rows // (count * SEGF), narrow, 0)
    functions = rows // SEGF
    total = lax.dot_general(
        jnp.ones((8, LANES), F32),
        part[...],
        (((1,), (1,)), ((), ())),
        precision=lax.Precision.HIGHEST,
        preferred_element_type=F32,
    )
    total = total * (1.0 / (SEGF * LANES))
    one = jnp.concatenate(
        [total[0:1, i * BLK : (i + 1) * BLK] for i in range(functions // BLK)]
        + [jnp.zeros((8 - functions // BLK, BLK), F32)],
        axis=0,
    )
    one = one.astype(BF16).astype(F32)
    for r in range(n_row):
        shift_ref[r] = one


def unpack(slot, ret, x, n_row):
    rows = x.shape[0]
    return pl.pallas_call(
        functools.partial(unpack_kernel, n_row),
        out_shape=(
            jax.ShapeDtypeStruct((rows, LANES), BF16),
            jax.ShapeDtypeStruct((n_row, 8, LANES), F32),
        ),
        in_specs=[SMEM, VMEM, VMEM],
        out_specs=(VMEM,) * 2,
        scratch_shapes=[
            pltpu.VMEM(ret.shape, F32),
            pltpu.VMEM((rows, LANES), F32),
            pltpu.VMEM((rows // SEGF, LANES), F32),
        ],
        compiler_params=params(20),
        cost_estimate=cost(10, 7 << 20),
        name="unpack",
    )(slot, ret, x)


def main_kernel(row_at, col_at, d_ref, *refs):
    bufs, (out_ref, sel, dcat) = refs[:-3], refs[-3:]
    rows, nnz = d_ref.shape[:2]
    width = nnz * BLK

    def one(i, carry):
        def clear(e, c):
            sel[pl.ds(pl.multiple_of(e * BLK, BLK), BLK), :] = jnp.zeros(
                (BLK, sel.shape[1]), BF16
            )
            return c

        lax.fori_loop(0, nnz, clear, 0)
        for e in range(nnz):
            dcat[:, e * BLK : (e + 1) * BLK] = d_ref[i, e]
        places = [(buf, j) for buf in bufs for j in range(buf.shape[0])]
        for q, (buf, j) in enumerate(places):
            e = row_at[i, q]

            @pl.when(e < nnz)
            def _():
                top = pl.multiple_of(e * BLK, BLK)

                def put(f, c):
                    g = col_at[i, q * nnz + f]
                    left = pl.multiple_of(g * BLK, BLK)
                    sel[pl.ds(top, BLK), pl.ds(left, BLK)] = buf[j, f]
                    return c

                lax.fori_loop(0, nnz, put, 0)

        def mult(n, c):
            at = pl.ds(pl.multiple_of(n * 256, 256), 256)
            out_ref[i, :, at] = jnp.dot(dcat[...], sel[:, at], preferred_element_type=F32)
            return c

        lax.fori_loop(0, width // 256, mult, 0)
        return carry

    lax.fori_loop(0, rows, one, 0)


def main_product(row_at, col_at, d, bufs):
    rows, nnz = d.shape[:2]
    return pl.pallas_call(
        main_kernel,
        out_shape=jax.ShapeDtypeStruct((rows, BLK, nnz * BLK), F32),
        in_specs=[SMEM, SMEM, VMEM] + [VMEM] * len(bufs),
        out_specs=VMEM,
        scratch_shapes=[
            pltpu.VMEM((nnz * BLK, (nnz + 1) * BLK), BF16),
            pltpu.VMEM((BLK, nnz * BLK), BF16),
        ],
        compiler_params=params(18),
        cost_estimate=cost(10, 10 << 20),
        name="hamiltonian",
    )(row_at, col_at, d, *bufs)


def final_kernel(at_ref, main_ref, d_ref, shift_ref, out_ref):
    rows, nnz = d_ref.shape[:2]
    for i in range(rows):
        for g in range(nnz):
            s = shift_ref[pl.ds(at_ref[i, g], 1), :]
            out_ref[i, g] = (
                main_ref[i, :, g * BLK : (g + 1) * BLK] + d_ref[i, g].astype(F32) * s
            ).astype(BF16)


def final(at, main, d, shift):
    return pl.pallas_call(
        final_kernel,
        out_shape=jax.ShapeDtypeStruct(d.shape, BF16),
        in_specs=[SMEM, VMEM, VMEM, VMEM],
        out_specs=VMEM,
        compiler_params=params(6),
        cost_estimate=cost(2, 4 << 20),
        name="final",
    )(at, main, d, shift)


ORDER = (0, 1, 3, 2)


def gather_hamiltonian(tiles, n_row):
    chips = n_row // 2
    assert chips == len(ORDER) and tiles.shape[0] == 2
    ahead = [(r, ((r // 2 + 1) % chips) * 2 + r % 2) for r in range(n_row)]
    behind = [(r, ((r // 2 - 1) % chips) * 2 + r % 2) for r in range(n_row)]
    one = lax.ppermute(tiles, "row", ahead)
    three = lax.ppermute(tiles, "row", behind)
    return one, three


def spread_hamiltonian(tiles, one, three, n_row):
    chips = n_row // 2
    ahead = [(r, ((r // 2 + 1) % chips) * 2 + r % 2) for r in range(n_row)]
    behind = [(r, ((r // 2 - 1) % chips) * 2 + r % 2) for r in range(n_row)]
    swap = [(r, r ^ 1) for r in range(n_row)]
    two_top = lax.ppermute(one[:1], "row", ahead)
    two_end = lax.ppermute(three[1:], "row", behind)
    same = [tiles, one, three, two_top, two_end]
    return same + [lax.ppermute(t, "row", swap) for t in same]


def positions(pattern, own_rows, n_row):
    me = lax.axis_index("row")
    chips = n_row // 2
    chip, core = me // 2, me % 2
    back = jnp.asarray(ORDER, jnp.int32)
    owner = (chip - back + chips) % chips * 2
    owner = jnp.concatenate([owner + core, owner + 1 - core])
    k = (owner[:, None] * own_rows + jnp.arange(own_rows, dtype=jnp.int32)).reshape(-1)
    own = lax.dynamic_slice_in_dim(pattern, me * own_rows, own_rows, 0)
    nnz = pattern.shape[1]
    local = own % (own_rows * n_row)
    index = jnp.arange(nnz, dtype=jnp.int32)
    row_at = jnp.min(
        jnp.where(local[:, None, :] == k[None, :, None], index, nnz), axis=2
    )
    rows = pattern[k]
    col_at = jnp.min(
        jnp.where(own[:, None, None, :] == rows[None, :, :, None], index, nnz), axis=3
    )
    shift_at = local // own_rows * 8 + local % own_rows
    return row_at, col_at.reshape(own_rows, -1), shift_at


def body(
    orbital_fragments,
    receiving_devices,
    fragment_grid_tile,
    outside_field_grid,
    density_matrix_tiles,
    energy_operator_tiles,
    tile_column_numbers,
):
    seg_dev = orbital_fragments.shape[0]
    n_orb = lax.axis_size("orb")
    n_row = lax.axis_size("row")
    devices = n_orb * n_row
    axes = ("orb", "row")

    def exchange(x):
        pairs = x.reshape(devices, -1, 2, LANES)
        got = lax.all_to_all(pairs, axes, split_axis=0, concat_axis=0, tiled=True)
        return got.reshape(-1, LANES)

    own_rows = density_matrix_tiles.shape[0]
    row_at, col_at, shift_at = positions(tile_column_numbers, own_rows, n_row)
    one, three = gather_hamiltonian(energy_operator_tiles, n_row)

    dest = receiving_devices.reshape(seg_dev // LANES, LANES)
    tile = fragment_grid_tile.reshape(seg_dev // LANES, LANES)
    me = (lax.axis_index("orb") * n_row + lax.axis_index("row")).reshape(1)
    slot, high, low = ranks(me, dest, tile, devices)
    slot = slot.reshape(seg_dev)
    outgoing = pack(slot, orbital_fragments, high, low)
    outgoing, one, three = lax.optimization_barrier((outgoing, one, three))
    arrived = exchange(outgoing)
    bufs = spread_hamiltonian(energy_operator_tiles, one, three, n_row)
    main = main_product(row_at, col_at, density_matrix_tiles, bufs)

    arrived, main = lax.optimization_barrier((arrived, main))
    results, charge = owner_step(arrived, outside_field_grid)
    applied, shift = unpack(slot, exchange(results), orbital_fragments, n_row)
    shift = lax.all_to_all(shift, "row", split_axis=0, concat_axis=0, tiled=True)
    product = final(shift_at, main, density_matrix_tiles, shift.reshape(n_row * 8, LANES))
    return (applied, charge, product)


def solution(mesh):
    return jax.shard_map(
        body,
        mesh=mesh,
        in_specs=(
            P(("orb", "row"), None),
            P(("orb", "row"), None),
            P(("orb", "row")),
            P(("orb", "row"), None),
            P(("orb", "row"), None, None, None),
            P(("orb", "row"), None, None, None),
            P("orb", None),
        ),
        out_specs=(
            P(("orb", "row"), None),
            P(("orb", "row"), None),
            P(("orb", "row"), None, None, None),
        ),
        check_vma=False,
    )
```

```python
import functools

import jax
import jax.numpy as jnp
from jax import lax
from jax.experimental import pallas as pl
from jax.experimental.pallas import tpu as pltpu
from jax.sharding import PartitionSpec as P

BLK = 128
SEGF = 24
CAP = 48
PAIR = 50
LANES = 128
F32 = jnp.float32
BF16 = jnp.bfloat16
VMEM = pl.BlockSpec(memory_space=pltpu.VMEM)
SMEM = pl.BlockSpec(memory_space=pltpu.SMEM)


def params(mib):
    return pltpu.CompilerParams(vmem_limit_bytes=mib << 20)


def cost(us, nbytes):
    return pl.CostEstimate(
        flops=int(us * 1e9), bytes_accessed=int(nbytes), transcendentals=0
    )


def iota(shape, axis):
    return lax.broadcasted_iota(jnp.int32, shape, axis)


def hot_rows(wide, which):
    return (wide == which).astype(F32).astype(BF16)


def columns(row):
    return jnp.transpose(jnp.broadcast_to(row, (LANES, LANES)))


def rank_kernel(devices, me_ref, dest_ref, tile_ref, slot_ref, back_ref, high_ref, low_ref, run, rank, acc):
    blocks = dest_ref.shape[0]
    group = 12
    owner = iota((devices, LANES), 0)
    lane = iota((16, LANES), 1)
    src, dst = iota((LANES, LANES), 0), iota((LANES, LANES), 1)
    ahead = src < dst
    run[...] = jnp.zeros_like(run)

    def count(q, c):
        hots, later = [], []
        for j in range(group):
            b = q * group + j
            d = dest_ref[pl.ds(b, 1), :]
            hots.append(hot_rows(owner, d))
            after = (lane > b).astype(F32).astype(BF16)
            later += [after] * (LANES // 16)
            same = (columns(d) == d) & ahead
            rank[pl.ds(b, 1), :] = jnp.sum(
                jnp.where(same, 1.0, 0.0), axis=0, keepdims=True
            )
        run[...] += jnp.dot(
            jnp.concatenate(hots, axis=1),
            jnp.concatenate(later, axis=0),
            preferred_element_type=F32,
        )
        return c

    lax.fori_loop(0, blocks // group, count, 0)
    totals = jnp.concatenate(
        [jnp.transpose(run[i : i + LANES, :]) for i in range(0, devices, LANES)], axis=1
    )
    acc[:LANES, :] = totals

    def order(q, c):
        for j in range(group):
            b = q * group + j
            d = dest_ref[pl.ds(b, 1), :]
            table = jnp.broadcast_to(acc[pl.ds(b, 1), :], (16, devices)).astype(BF16)
            before = jnp.dot(table, hot_rows(owner, d), preferred_element_type=F32)
            mine = (before[0:1] + rank[pl.ds(b, 1), :]).astype(jnp.int32)
            rank[pl.ds(b, 1), :] = mine.astype(F32)
            slot_ref[pl.ds(b, 1), :] = d * PAIR + mine
            back_ref[pl.ds(b, 1), :] = d * CAP + mine
        return c

    lax.fori_loop(0, blocks // group, order, 0)
    turn = me_ref[0] * PAIR
    acc[...] = jnp.zeros_like(acc)

    def mark(q, c):
        hots, spreads = [], []
        for j in range(group):
            b = q * group + j
            hots.append(hot_rows(owner, dest_ref[pl.ds(b, 1), :]))
            place = rank[pl.ds(b, 1), :].astype(jnp.int32) + turn
            at = src == (place & (LANES - 1))
            label = tile_ref[pl.ds(b, 1), :] + 1
            high = jnp.where(at, (label >> 2).astype(F32), 0.0)
            low = jnp.where(at, (label & 3).astype(F32), 0.0)
            spreads.append(jnp.concatenate([high, low], axis=0).astype(BF16))
        acc[...] += lax.dot_general(
            jnp.concatenate(hots, axis=1),
            jnp.concatenate(spreads, axis=1),
            (((1,), (1,)), ((), ())),
            preferred_element_type=F32,
        )
        return c

    lax.fori_loop(0, blocks // group, mark, 0)
    high_ref[...] = acc[:, :LANES]
    low_ref[...] = acc[:, LANES:]


def ranks(me, dest, tile, devices):
    blocks = dest.shape[0]
    return pl.pallas_call(
        functools.partial(rank_kernel, devices),
        out_shape=(
            jax.ShapeDtypeStruct((blocks, LANES), jnp.int32),
            jax.ShapeDtypeStruct((blocks, LANES), jnp.int32),
            jax.ShapeDtypeStruct((devices, LANES), F32),
            jax.ShapeDtypeStruct((devices, LANES), F32),
        ),
        in_specs=[SMEM, VMEM, VMEM],
        out_specs=(VMEM,) * 4,
        scratch_shapes=[
            pltpu.VMEM((devices, LANES), F32),
            pltpu.VMEM((blocks, LANES), F32),
            pltpu.VMEM((devices, 2 * LANES), F32),
        ],
        compiler_params=params(5),
        cost_estimate=cost(4, 1 << 18),
        name="rank",
    )(me, dest, tile)


ROWS = 64


def widen(src_ref, dst):
    def step(i, c):
        at = pl.ds(pl.multiple_of(i * 256, 256), 256)
        dst[at, :] = src_ref[at, :].astype(F32)
        return c

    lax.fori_loop(0, src_ref.shape[0] // 256, step, 0)


def pack_kernel(slot_ref, x_ref, high_ref, low_ref, out_ref, xf, of):
    rows = x_ref.shape[0]
    slots = of.shape[0]
    devices = high_ref.shape[0]
    widen(x_ref, xf)

    def clear(i, c):
        of[pl.ds(pl.multiple_of(i * 512, 512), 512), :] = jnp.zeros((512, LANES), F32)
        return c

    lax.fori_loop(0, slots // 512, clear, 0)

    def move(i, c):
        base = pl.multiple_of(i * ROWS, ROWS)
        here = slot_ref.at[pl.ds(base, ROWS)]
        rows_in = xf.at[pl.ds(base, ROWS)]
        for j in range(ROWS):
            of[pl.ds(here[j], 1), :] = rows_in[j : j + 1, :]
        return c

    lax.fori_loop(0, rows // ROWS, move, 0)
    of[pl.ds(CAP, devices, stride=PAIR), :] = high_ref[...]
    of[pl.ds(CAP + 1, devices, stride=PAIR), :] = low_ref[...]

    def narrow(i, c):
        at = pl.ds(pl.multiple_of(i * 256, 256), 256)
        out_ref[at, :] = of[at, :].astype(BF16)
        return c

    lax.fori_loop(0, slots // 256, narrow, 0)


def pack(slot, x, high, low):
    rows = x.shape[0]
    slots = high.shape[0] * PAIR
    return pl.pallas_call(
        pack_kernel,
        out_shape=jax.ShapeDtypeStruct((slots, LANES), BF16),
        in_specs=[SMEM, VMEM, VMEM, VMEM],
        out_specs=VMEM,
        scratch_shapes=[pltpu.VMEM((rows, LANES), F32), pltpu.VMEM((slots, LANES), F32)],
        compiler_params=params(18),
        cost_estimate=cost(10, 5 << 20),
        name="pack",
    )(slot, x, high, low)


DEPTH = 1280
CHUNK = 1280


def slot_labels(high, low):
    devices = high.shape[0]
    groups = -(-devices * PAIR // LANES // 8) * 8
    source, lane = iota((devices, LANES), 0), iota((devices, LANES), 1)
    offset = (source * PAIR) & (LANES - 1)
    near = lane >= offset
    k, s = iota((groups, devices), 0), iota((groups, devices), 1)
    first = (s * PAIR) >> 7
    left = jnp.concatenate([first == k, first + 1 == k], axis=1)
    left = left.astype(F32).astype(BF16)

    def part(x):
        return jnp.concatenate(
            [jnp.where(near, x, 0.0), jnp.where(near, 0.0, x)], axis=0
        ).astype(BF16)

    right = jnp.concatenate([part(high), part(low)], axis=1)
    both = jnp.dot(left, right, preferred_element_type=F32)
    return (both[:, :LANES] * 4.0 + both[:, LANES:]).astype(jnp.int32) - 1


def owner_kernel(v_ref, field_hbm, out_ref, charge_ref, vf, label, acc, pot, field_ref, sem):
    slots = v_ref.shape[0]
    tiles = charge_ref.shape[0]
    devices = slots // PAIR
    fetch = pltpu.make_async_copy(field_hbm, field_ref, sem)
    fetch.start()
    widen(v_ref, vf)
    label[...] = slot_labels(
        vf[pl.ds(CAP, devices, stride=PAIR), :],
        vf[pl.ds(CAP + 1, devices, stride=PAIR), :],
    )
    acc[...] = jnp.zeros_like(acc)
    cell = iota((tiles, LANES), 0)

    def add(k, c):
        hot = []
        for j in range(DEPTH // LANES):
            hot.append(hot_rows(cell, label[pl.ds(k * (DEPTH // LANES) + j, 1), :]))
        v = vf[pl.ds(pl.multiple_of(k * DEPTH, DEPTH), DEPTH), :]
        square = v * v
        high = square.astype(BF16)
        low = (square - high.astype(F32)).astype(BF16)
        acc[...] += jnp.dot(
            jnp.concatenate(hot, axis=1),
            jnp.concatenate([high, low], axis=1),
            preferred_element_type=F32,
        )
        return c

    lax.fori_loop(0, slots // DEPTH, add, 0)
    charge = acc[:, :LANES] + acc[:, LANES:]
    charge_ref[...] = charge
    fetch.wait()
    field = field_ref[...] - 1.5 * jnp.exp(jnp.log(1.0 + charge) * (1.0 / 3.0))
    high = field.astype(BF16)
    pot[:, :LANES] = high
    pot[:, LANES:] = (field - high.astype(F32)).astype(BF16)
    lane = iota((LANES, tiles), 1)

    def apply(k, c):
        hot = []
        for j in range(CHUNK // LANES):
            col = columns(label[pl.ds(k * (CHUNK // LANES) + j, 1), :])
            hot.append(hot_rows(lane, jnp.concatenate([col] * (tiles // LANES), axis=1)))
        got = jnp.dot(
            jnp.concatenate(hot, axis=0), pot[...], preferred_element_type=F32
        )
        at = pl.ds(pl.multiple_of(k * CHUNK, CHUNK), CHUNK)
        here = got[:, :LANES] + got[:, LANES:]
        vf[at, :] = here * vf[at, :]
        return c

    lax.fori_loop(0, slots // CHUNK, apply, 0)
    pairs = 8

    def narrow(i, c):
        source = vf.at[pl.ds(pl.multiple_of(i * pairs * PAIR, 8), pairs * PAIR)]
        at = pl.ds(pl.multiple_of(i * pairs * CAP, pairs * CAP), pairs * CAP)
        out_ref[at, :] = jnp.concatenate(
            [source[j * PAIR : j * PAIR + CAP, :] for j in range(pairs)], axis=0
        ).astype(BF16)
        return c

    lax.fori_loop(0, devices // pairs, narrow, 0)


def owner_step(v, field):
    slots = v.shape[0]
    tiles = field.shape[0]
    return pl.pallas_call(
        owner_kernel,
        out_shape=(
            jax.ShapeDtypeStruct((slots // PAIR * CAP, LANES), BF16),
            jax.ShapeDtypeStruct((tiles, LANES), F32),
        ),
        in_specs=[VMEM, pl.BlockSpec(memory_space=pl.ANY)],
        out_specs=(VMEM,) * 2,
        scratch_shapes=[
            pltpu.VMEM((slots, LANES), F32),
            pltpu.VMEM((-(-slots // LANES // 8) * 8, LANES), jnp.int32),
            pltpu.VMEM((tiles, 2 * LANES), F32),
            pltpu.VMEM((tiles, 2 * LANES), BF16),
            pltpu.VMEM((tiles, LANES), F32),
            pltpu.SemaphoreType.DMA,
        ],
        compiler_params=params(28),
        cost_estimate=cost(16, 7 << 20),
        name="owner",
    )(v, field)


def unpack_kernel(n_row, slot_ref, ret_ref, x_ref, out_ref, shift_ref, rf, of, part):
    rows = x_ref.shape[0]
    widen(ret_ref, rf)

    def move(i, c):
        base = pl.multiple_of(i * ROWS, ROWS)
        here = slot_ref.at[pl.ds(base, ROWS)]
        rows_out = of.at[pl.ds(base, ROWS)]
        for j in range(ROWS):
            rows_out[j : j + 1, :] = rf[pl.ds(here[j], 1), :]
        return c

    lax.fori_loop(0, rows // ROWS, move, 0)
    count = 8

    def narrow(i, c):
        at = pl.ds(pl.multiple_of(i * count * SEGF, count * SEGF), count * SEGF)
        got = of[at, :]
        out_ref[at, :] = got.astype(BF16)
        work = (got * x_ref[at, :].astype(F32)).reshape(count, SEGF, LANES)
        part[pl.ds(pl.multiple_of(i * count, count), count), :] = jnp.sum(work, axis=1)
        return c

    lax.fori_loop(0, rows // (count * SEGF), narrow, 0)
    functions = rows // SEGF
    total = lax.dot_general(
        jnp.ones((8, LANES), F32),
        part[...],
        (((1,), (1,)), ((), ())),
        precision=lax.Precision.HIGHEST,
        preferred_element_type=F32,
    )
    total = total * (1.0 / (SEGF * LANES))
    one = jnp.concatenate(
        [total[0:1, i * BLK : (i + 1) * BLK] for i in range(functions // BLK)]
        + [jnp.zeros((8 - functions // BLK, BLK), F32)],
        axis=0,
    )
    one = one.astype(BF16).astype(F32)
    for r in range(n_row):
        shift_ref[r] = one


def unpack(slot, ret, x, n_row):
    rows = x.shape[0]
    return pl.pallas_call(
        functools.partial(unpack_kernel, n_row),
        out_shape=(
            jax.ShapeDtypeStruct((rows, LANES), BF16),
            jax.ShapeDtypeStruct((n_row, 8, LANES), F32),
        ),
        in_specs=[SMEM, VMEM, VMEM],
        out_specs=(VMEM,) * 2,
        scratch_shapes=[
            pltpu.VMEM(ret.shape, F32),
            pltpu.VMEM((rows, LANES), F32),
            pltpu.VMEM((rows // SEGF, LANES), F32),
        ],
        compiler_params=params(20),
        cost_estimate=cost(10, 7 << 20),
        name="unpack",
    )(slot, ret, x)


def main_kernel(row_at, col_at, d_ref, *refs):
    bufs, (out_ref, sel, dcat) = refs[:-3], refs[-3:]
    rows, nnz = d_ref.shape[:2]
    width = nnz * BLK

    def one(i, carry):
        def clear(e, c):
            sel[pl.ds(pl.multiple_of(e * BLK, BLK), BLK), :] = jnp.zeros(
                (BLK, sel.shape[1]), BF16
            )
            return c

        lax.fori_loop(0, nnz, clear, 0)
        for e in range(nnz):
            dcat[:, e * BLK : (e + 1) * BLK] = d_ref[i, e]
        places = [(buf, j) for buf in bufs for j in range(buf.shape[0])]
        for q, (buf, j) in enumerate(places):
            e = row_at[i, q]

            @pl.when(e < nnz)
            def _():
                top = pl.multiple_of(e * BLK, BLK)

                def put(f, c):
                    g = col_at[i, q * nnz + f]
                    left = pl.multiple_of(g * BLK, BLK)
                    sel[pl.ds(top, BLK), pl.ds(left, BLK)] = buf[j, f]
                    return c

                lax.fori_loop(0, nnz, put, 0)

        def mult(n, c):
            at = pl.ds(pl.multiple_of(n * 256, 256), 256)
            out_ref[i, :, at] = jnp.dot(dcat[...], sel[:, at], preferred_element_type=F32)
            return c

        lax.fori_loop(0, width // 256, mult, 0)
        return carry

    lax.fori_loop(0, rows, one, 0)


def main_product(row_at, col_at, d, bufs):
    rows, nnz = d.shape[:2]
    return pl.pallas_call(
        main_kernel,
        out_shape=jax.ShapeDtypeStruct((rows, BLK, nnz * BLK), F32),
        in_specs=[SMEM, SMEM, VMEM] + [VMEM] * len(bufs),
        out_specs=VMEM,
        scratch_shapes=[
            pltpu.VMEM((nnz * BLK, (nnz + 1) * BLK), BF16),
            pltpu.VMEM((BLK, nnz * BLK), BF16),
        ],
        compiler_params=params(18),
        cost_estimate=cost(10, 10 << 20),
        name="hamiltonian",
    )(row_at, col_at, d, *bufs)


def final_kernel(at_ref, main_ref, d_ref, shift_ref, out_ref):
    rows, nnz = d_ref.shape[:2]
    for i in range(rows):
        for g in range(nnz):
            s = shift_ref[pl.ds(at_ref[i, g], 1), :]
            out_ref[i, g] = (
                main_ref[i, :, g * BLK : (g + 1) * BLK] + d_ref[i, g].astype(F32) * s
            ).astype(BF16)


def final(at, main, d, shift):
    return pl.pallas_call(
        final_kernel,
        out_shape=jax.ShapeDtypeStruct(d.shape, BF16),
        in_specs=[SMEM, VMEM, VMEM, VMEM],
        out_specs=VMEM,
        compiler_params=params(6),
        cost_estimate=cost(2, 4 << 20),
        name="final",
    )(at, main, d, shift)


ORDER = (0, 1, 3, 2)


def gather_hamiltonian(tiles, n_row):
    chips = n_row // 2
    assert chips == len(ORDER) and tiles.shape[0] == 2
    ahead = [(r, ((r // 2 + 1) % chips) * 2 + r % 2) for r in range(n_row)]
    behind = [(r, ((r // 2 - 1) % chips) * 2 + r % 2) for r in range(n_row)]
    one = lax.ppermute(tiles, "row", ahead)
    three = lax.ppermute(tiles, "row", behind)
    return one, three


def spread_hamiltonian(tiles, one, three, n_row):
    chips = n_row // 2
    ahead = [(r, ((r // 2 + 1) % chips) * 2 + r % 2) for r in range(n_row)]
    behind = [(r, ((r // 2 - 1) % chips) * 2 + r % 2) for r in range(n_row)]
    swap = [(r, r ^ 1) for r in range(n_row)]
    two_top = lax.ppermute(one[:1], "row", ahead)
    two_end = lax.ppermute(three[1:], "row", behind)
    same = [tiles, one, three, two_top, two_end]
    return same + [lax.ppermute(t, "row", swap) for t in same]


def positions(pattern, own_rows, n_row):
    me = lax.axis_index("row")
    chips = n_row // 2
    chip, core = me // 2, me % 2
    back = jnp.asarray(ORDER, jnp.int32)
    owner = (chip - back + chips) % chips * 2
    owner = jnp.concatenate([owner + core, owner + 1 - core])
    k = (owner[:, None] * own_rows + jnp.arange(own_rows, dtype=jnp.int32)).reshape(-1)
    own = lax.dynamic_slice_in_dim(pattern, me * own_rows, own_rows, 0)
    nnz = pattern.shape[1]
    local = own % (own_rows * n_row)
    index = jnp.arange(nnz, dtype=jnp.int32)
    row_at = jnp.min(
        jnp.where(local[:, None, :] == k[None, :, None], index, nnz), axis=2
    )
    rows = pattern[k]
    col_at = jnp.min(
        jnp.where(own[:, None, None, :] == rows[None, :, :, None], index, nnz), axis=3
    )
    shift_at = local // own_rows * 8 + local % own_rows
    return row_at, col_at.reshape(own_rows, -1), shift_at


def body(
    orbital_fragments,
    receiving_devices,
    fragment_grid_tile,
    outside_field_grid,
    density_matrix_tiles,
    energy_operator_tiles,
    tile_column_numbers,
):
    seg_dev = orbital_fragments.shape[0]
    n_orb = lax.axis_size("orb")
    n_row = lax.axis_size("row")
    devices = n_orb * n_row
    axes = ("orb", "row")

    def exchange(x, *block):
        pairs = x.reshape(devices, *block, LANES)
        got = lax.all_to_all(pairs, axes, split_axis=0, concat_axis=0, tiled=True)
        return got.reshape(-1, LANES)

    own_rows = density_matrix_tiles.shape[0]
    row_at, col_at, shift_at = positions(tile_column_numbers, own_rows, n_row)
    one, three = gather_hamiltonian(energy_operator_tiles, n_row)

    dest = receiving_devices.reshape(seg_dev // LANES, LANES)
    tile = fragment_grid_tile.reshape(seg_dev // LANES, LANES)
    me = (lax.axis_index("orb") * n_row + lax.axis_index("row")).reshape(1)
    slot, back, high, low = ranks(me, dest, tile, devices)
    slot, back = slot.reshape(seg_dev), back.reshape(seg_dev)
    outgoing = pack(slot, orbital_fragments, high, low)
    outgoing, one, three = lax.optimization_barrier((outgoing, one, three))
    arrived = exchange(outgoing, PAIR // 2, 2)
    bufs = spread_hamiltonian(energy_operator_tiles, one, three, n_row)
    main = main_product(row_at, col_at, density_matrix_tiles, bufs)

    arrived, main = lax.optimization_barrier((arrived, main))
    results, charge = owner_step(arrived, outside_field_grid)
    applied, shift = unpack(back, exchange(results, CAP), orbital_fragments, n_row)
    shift = lax.all_to_all(shift, "row", split_axis=0, concat_axis=0, tiled=True)
    product = final(shift_at, main, density_matrix_tiles, shift.reshape(n_row * 8, LANES))
    return (applied, charge, product)


def solution(mesh):
    return jax.shard_map(
        body,
        mesh=mesh,
        in_specs=(
            P(("orb", "row"), None),
            P(("orb", "row"), None),
            P(("orb", "row")),
            P(("orb", "row"), None),
            P(("orb", "row"), None, None, None),
            P(("orb", "row"), None, None, None),
            P("orb", None),
        ),
        out_specs=(
            P(("orb", "row"), None),
            P(("orb", "row"), None),
            P(("orb", "row"), None, None, None),
        ),
        check_vma=False,
    )
```

```python
import functools

import jax
import jax.numpy as jnp
from jax import lax
from jax.experimental import pallas as pl
from jax.experimental.pallas import tpu as pltpu
from jax.sharding import PartitionSpec as P

BLK = 128
SEGF = 24
CAP = 48
PAIR = 50
LANES = 128
F32 = jnp.float32
BF16 = jnp.bfloat16
VMEM = pl.BlockSpec(memory_space=pltpu.VMEM)
SMEM = pl.BlockSpec(memory_space=pltpu.SMEM)


def params(mib):
    return pltpu.CompilerParams(vmem_limit_bytes=int(mib * 1024) << 10)


def cost(us, nbytes):
    return pl.CostEstimate(
        flops=int(us * 1e9), bytes_accessed=int(nbytes), transcendentals=0
    )


def iota(shape, axis):
    return lax.broadcasted_iota(jnp.int32, shape, axis)


def hot_rows(wide, which):
    return (wide == which).astype(F32).astype(BF16)


def columns(row):
    return jnp.transpose(jnp.broadcast_to(row, (LANES, LANES)))


ROWS = 64
ANY = pl.BlockSpec(memory_space=pltpu.HBM)


def widen(src_ref, dst):
    def step(i, c):
        at = pl.ds(pl.multiple_of(i * 256, 256), 256)
        dst[at, :] = src_ref[at, :].astype(F32)
        return c

    lax.fori_loop(0, src_ref.shape[0] // 256, step, 0)


STRIP = 8


def index_copies(slot_ref, regions, sems, strip):
    return [
        pltpu.make_async_copy(
            slot_ref.at[pl.ds(pl.multiple_of((strip + r) * STRIP, STRIP), STRIP)],
            region,
            sems.at[r],
        )
        for r, region in enumerate(regions)
    ]


def load_index(slot_ref, regions, sems, strip):
    for copy in index_copies(slot_ref, regions, sems, strip):
        copy.start()


def by_strips(slot_ref, regions, sems, work):
    strips = slot_ref.shape[0] // STRIP
    count = len(regions)

    def step(q, c):
        copies = index_copies(slot_ref, regions, sems, q * count)
        later = index_copies(slot_ref, regions, sems, (q + 1) * count)
        for r, region in enumerate(regions):
            copies[r].wait()
            first = pl.multiple_of((q * count + r) * STRIP * LANES, STRIP * LANES)
            work(first, lambda i: region[i // LANES, i % LANES])

            @pl.when((q + 1) * count < strips)
            def _():
                later[r].start()

        return c

    lax.fori_loop(0, strips // count, step, 0)


def send_kernel(
    devices,
    me_ref,
    dest_hbm,
    tile_hbm,
    x_hbm,
    out_hbm,
    back_ref,
    dest_ref,
    tile_ref,
    x_ref,
    run,
    rank,
    acc,
    slot_ref,
    smem0,
    smem1,
    xf,
    of,
    out_ref,
    sems,
    out_sems,
):
    loads = [
        pltpu.make_async_copy(src, dst, sems.at[i])
        for i, (src, dst) in enumerate(
            [(dest_hbm, dest_ref), (tile_hbm, tile_ref), (x_hbm, x_ref)]
        )
    ]
    for load in loads:
        load.start()
    blocks = dest_ref.shape[0]
    slots = of.shape[0]
    group = 12
    steps = blocks // group
    owner = iota((devices, LANES), 0)
    lane = iota((16, LANES), 1)
    src, dst = iota((LANES, LANES), 0), iota((LANES, LANES), 1)
    ahead = src < dst
    run[...] = jnp.zeros_like(run)
    loads[0].wait()

    def count(q, c):
        part = slots // steps
        of[pl.ds(pl.multiple_of(q * part, 128), part), :] = jnp.zeros((part, LANES), F32)
        hots, later = [], []
        for j in range(group):
            b = q * group + j
            d = dest_ref[pl.ds(b, 1), :]
            hots.append(hot_rows(owner, d))
            after = (lane > b).astype(F32).astype(BF16)
            later += [after] * (LANES // 16)
            same = (columns(d) == d) & ahead
            rank[pl.ds(b, 1), :] = jnp.sum(
                jnp.where(same, 1.0, 0.0), axis=0, keepdims=True
            )
        run[...] += jnp.dot(
            jnp.concatenate(hots, axis=1),
            jnp.concatenate(later, axis=0),
            preferred_element_type=F32,
        )
        return c

    lax.fori_loop(0, steps, count, 0)
    acc[:LANES, :] = jnp.concatenate(
        [jnp.transpose(run[i : i + LANES, :]) for i in range(0, devices, LANES)], axis=1
    )
    loads[1].wait()
    loads[2].wait()

    def order(q, c):
        part = group * LANES
        rows = pl.ds(pl.multiple_of(q * part, part), part)
        xf[rows, :] = x_ref[rows, :].astype(F32)
        for j in range(group):
            b = q * group + j
            d = dest_ref[pl.ds(b, 1), :]
            table = jnp.broadcast_to(acc[pl.ds(b, 1), :], (16, devices)).astype(BF16)
            before = jnp.dot(table, hot_rows(owner, d), preferred_element_type=F32)
            mine = (before[0:1] + rank[pl.ds(b, 1), :]).astype(jnp.int32)
            rank[pl.ds(b, 1), :] = mine.astype(F32)
            slot_ref[pl.ds(b, 1), :] = d * PAIR + mine
            back_ref[pl.ds(b, 1), :] = d * CAP + mine
        return c

    lax.fori_loop(0, steps, order, 0)
    regions = (smem0, smem1)
    index_sems = sems.at[pl.ds(3, 2)]
    load_index(slot_ref, regions, index_sems, 0)
    turn = me_ref[0] * PAIR
    acc[...] = jnp.zeros_like(acc)
    few = 4

    def mark(first):
        hots, spreads = [], []
        for j in range(few):
            b = first + j
            hots.append(hot_rows(owner, dest_ref[pl.ds(b, 1), :]))
            place = rank[pl.ds(b, 1), :].astype(jnp.int32) + turn
            at = src == (place & (LANES - 1))
            label = tile_ref[pl.ds(b, 1), :] + 1
            high = jnp.where(at, (label >> 2).astype(F32), 0.0)
            low = jnp.where(at, (label & 3).astype(F32), 0.0)
            spreads.append(jnp.concatenate([high, low], axis=0).astype(BF16))
        acc[...] += lax.dot_general(
            jnp.concatenate(hots, axis=1),
            jnp.concatenate(spreads, axis=1),
            (((1,), (1,)), ((), ())),
            preferred_element_type=F32,
        )

    def move(first, place):
        here = xf.at[pl.ds(first, STRIP * LANES)]
        block = first // LANES
        for q in range(STRIP // few):
            mark(block + q * few)
            for i in range(q * few * LANES, (q + 1) * few * LANES):
                of[pl.ds(place(i), 1), :] = here[i : i + 1, :]

    by_strips(slot_ref, regions, index_sems, move)
    of[pl.ds(CAP, devices, stride=PAIR), :] = acc[:, :LANES]
    of[pl.ds(CAP + 1, devices, stride=PAIR), :] = acc[:, LANES:]
    for copy in put_out(lambda at: of[at, :], out_ref, out_hbm, out_sems, 320):
        copy.wait()


def put_out(get, out_ref, out_hbm, sems, size):
    pieces = sems.shape[0]
    part = out_ref.shape[0] // pieces
    copies = []
    for p in range(pieces):

        def narrow(i, c):
            at = pl.ds(pl.multiple_of(p * part + i * size, size), size)
            out_ref[at, :] = get(at).astype(BF16)
            return c

        lax.fori_loop(0, part // size, narrow, 0)
        at = pl.ds(p * part, part)
        copies.append(
            pltpu.make_async_copy(out_ref.at[at], out_hbm.at[at], sems.at[p])
        )
        copies[-1].start()
    return copies


def send_side(me, dest, tile, x, devices):
    blocks = dest.shape[0]
    slots = devices * PAIR
    return pl.pallas_call(
        functools.partial(send_kernel, devices),
        out_shape=(
            jax.ShapeDtypeStruct((slots, LANES), BF16),
            jax.ShapeDtypeStruct((blocks, LANES), jnp.int32),
        ),
        in_specs=[SMEM, ANY, ANY, ANY],
        out_specs=(ANY, VMEM),
        scratch_shapes=[
            pltpu.VMEM((blocks, LANES), jnp.int32),
            pltpu.VMEM((blocks, LANES), jnp.int32),
            pltpu.VMEM(x.shape, BF16),
            pltpu.VMEM((devices, LANES), F32),
            pltpu.VMEM((blocks, LANES), F32),
            pltpu.VMEM((devices, 2 * LANES), F32),
            pltpu.VMEM((blocks, LANES), jnp.int32),
            pltpu.SMEM((STRIP, LANES), jnp.int32),
            pltpu.SMEM((STRIP, LANES), jnp.int32),
            pltpu.VMEM(x.shape, F32),
            pltpu.VMEM((slots, LANES), F32),
            pltpu.VMEM((slots, LANES), BF16),
            pltpu.SemaphoreType.DMA((5,)),
            pltpu.SemaphoreType.DMA((5,)),
        ],
        compiler_params=params(61),
        cost_estimate=cost(12, 5 << 20),
        name="send",
    )(me, dest, tile, x)


OWNER = 28
DEPTH = 1280
CHUNK = 1280


def slot_labels(high, low):
    devices = high.shape[0]
    groups = -(-devices * PAIR // LANES // 8) * 8
    source, lane = iota((devices, LANES), 0), iota((devices, LANES), 1)
    offset = (source * PAIR) & (LANES - 1)
    near = lane >= offset
    k, s = iota((groups, devices), 0), iota((groups, devices), 1)
    first = (s * PAIR) >> 7
    left = jnp.concatenate([first == k, first + 1 == k], axis=1)
    left = left.astype(F32).astype(BF16)

    def part(x):
        return jnp.concatenate(
            [jnp.where(near, x, 0.0), jnp.where(near, 0.0, x)], axis=0
        ).astype(BF16)

    right = jnp.concatenate([part(high), part(low)], axis=1)
    both = jnp.dot(left, right, preferred_element_type=F32)
    return (both[:, :LANES] * 4.0 + both[:, LANES:]).astype(jnp.int32) - 1


def owner_kernel(
    v_ref,
    field_hbm,
    out_hbm,
    charge_ref,
    vf,
    label,
    acc,
    pot,
    field_ref,
    out_ref,
    sem,
    out_sems,
):
    slots = v_ref.shape[0]
    tiles = charge_ref.shape[0]
    devices = slots // PAIR
    fetch = pltpu.make_async_copy(field_hbm, field_ref, sem)
    fetch.start()
    acc[...] = jnp.zeros_like(acc)
    widen(v_ref, vf)
    label[...] = slot_labels(
        vf[pl.ds(CAP, devices, stride=PAIR), :],
        vf[pl.ds(CAP + 1, devices, stride=PAIR), :],
    )
    cell = iota((tiles, LANES), 0)

    def add(k, c):
        hot = []
        for j in range(DEPTH // LANES):
            hot.append(hot_rows(cell, label[pl.ds(k * (DEPTH // LANES) + j, 1), :]))
        v = vf[pl.ds(pl.multiple_of(k * DEPTH, DEPTH), DEPTH), :]
        square = v * v
        high = square.astype(BF16)
        low = (square - high.astype(F32)).astype(BF16)
        acc[...] += jnp.dot(
            jnp.concatenate(hot, axis=1),
            jnp.concatenate([high, low], axis=1),
            preferred_element_type=F32,
        )
        return c

    lax.fori_loop(0, slots // DEPTH, add, 0)
    charge = acc[:, :LANES] + acc[:, LANES:]
    charge_ref[...] = charge
    fetch.wait()
    field = field_ref[...] - 1.5 * jnp.exp(jnp.log(1.0 + charge) * (1.0 / 3.0))
    high = field.astype(BF16)
    pot[:, :LANES] = high
    pot[:, LANES:] = (field - high.astype(F32)).astype(BF16)
    lane = iota((LANES, tiles), 1)

    def apply(k, c):
        hot = []
        for j in range(CHUNK // LANES):
            col = columns(label[pl.ds(k * (CHUNK // LANES) + j, 1), :])
            hot.append(hot_rows(lane, jnp.concatenate([col] * (tiles // LANES), axis=1)))
        got = jnp.dot(
            jnp.concatenate(hot, axis=0), pot[...], preferred_element_type=F32
        )
        at = pl.ds(pl.multiple_of(k * CHUNK, CHUNK), CHUNK)
        here = got[:, :LANES] + got[:, LANES:]
        vf[at, :] = here * vf[at, :]
        return c

    lax.fori_loop(0, slots // CHUNK, apply, 0)
    pairs = 8

    def without_labels(at):
        first = pl.multiple_of(at.start // CAP * PAIR, 8)
        source = vf.at[pl.ds(first, pairs * PAIR)]
        return jnp.concatenate(
            [source[j * PAIR : j * PAIR + CAP, :] for j in range(pairs)], axis=0
        )

    for copy in put_out(without_labels, out_ref, out_hbm, out_sems, pairs * CAP):
        copy.wait()


def owner_step(v, field):
    slots = v.shape[0]
    tiles = field.shape[0]
    return pl.pallas_call(
        owner_kernel,
        out_shape=(
            jax.ShapeDtypeStruct((slots // PAIR * CAP, LANES), BF16),
            jax.ShapeDtypeStruct((tiles, LANES), F32),
        ),
        in_specs=[VMEM, ANY],
        out_specs=(ANY, VMEM),
        scratch_shapes=[
            pltpu.VMEM((slots, LANES), F32),
            pltpu.VMEM((-(-slots // LANES // 8) * 8, LANES), jnp.int32),
            pltpu.VMEM((tiles, 2 * LANES), F32),
            pltpu.VMEM((tiles, 2 * LANES), BF16),
            pltpu.VMEM((tiles, LANES), F32),
            pltpu.VMEM((slots // PAIR * CAP, LANES), BF16),
            pltpu.SemaphoreType.DMA,
            pltpu.SemaphoreType.DMA((4,)),
        ],
        compiler_params=params(OWNER),
        cost_estimate=cost(16, 7 << 20),
        name="owner",
    )(v, field)


def unpack_kernel(
    n_row,
    slot_ref,
    ret_ref,
    x_ref,
    out_hbm,
    shift_ref,
    rf,
    of,
    part,
    out_ref,
    smem0,
    smem1,
    sems,
    out_sems,
):
    rows = x_ref.shape[0]
    regions = (smem0, smem1)
    load_index(slot_ref, regions, sems, 0)
    widen(ret_ref, rf)

    def take(first, place):
        rows_out = of.at[pl.ds(first, STRIP * LANES)]
        for i in range(STRIP * LANES):
            rows_out[i : i + 1, :] = rf[pl.ds(place(i), 1), :]

    by_strips(slot_ref, regions, sems, take)
    count = 8

    def with_shift(at):
        got = of[at, :]
        work = (got * x_ref[at, :].astype(F32)).reshape(count, SEGF, LANES)
        first = pl.multiple_of(at.start // SEGF, count)
        part[pl.ds(first, count), :] = jnp.sum(work, axis=1)
        return got

    copies = put_out(with_shift, out_ref, out_hbm, out_sems, count * SEGF)
    functions = rows // SEGF
    total = lax.dot_general(
        jnp.ones((8, LANES), F32),
        part[...],
        (((1,), (1,)), ((), ())),
        precision=lax.Precision.HIGHEST,
        preferred_element_type=F32,
    )
    total = total * (1.0 / (SEGF * LANES))
    one = jnp.concatenate(
        [total[0:1, i * BLK : (i + 1) * BLK] for i in range(functions // BLK)]
        + [jnp.zeros((8 - functions // BLK, BLK), F32)],
        axis=0,
    )
    one = one.astype(BF16).astype(F32)
    for r in range(n_row):
        shift_ref[r] = one
    for copy in copies:
        copy.wait()


def unpack(slot, ret, x, n_row):
    rows = x.shape[0]
    return pl.pallas_call(
        functools.partial(unpack_kernel, n_row),
        out_shape=(
            jax.ShapeDtypeStruct((rows, LANES), BF16),
            jax.ShapeDtypeStruct((n_row, 8, LANES), F32),
        ),
        in_specs=[VMEM, VMEM, VMEM],
        out_specs=(ANY, VMEM),
        scratch_shapes=[
            pltpu.VMEM(ret.shape, F32),
            pltpu.VMEM((rows, LANES), F32),
            pltpu.VMEM((rows // SEGF, LANES), F32),
            pltpu.VMEM((rows, LANES), BF16),
            pltpu.SMEM((STRIP, LANES), jnp.int32),
            pltpu.SMEM((STRIP, LANES), jnp.int32),
            pltpu.SemaphoreType.DMA((2,)),
            pltpu.SemaphoreType.DMA((4,)),
        ],
        compiler_params=params(20),
        cost_estimate=cost(10, 7 << 20),
        name="unpack",
    )(slot, ret, x)


def main_kernel(row_at, col_at, d_ref, *refs):
    bufs, (out_ref, sel, dcat) = refs[:-3], refs[-3:]
    rows, nnz = d_ref.shape[:2]
    width = nnz * BLK

    def one(i, carry):
        def clear(e, c):
            sel[pl.ds(pl.multiple_of(e * BLK, BLK), BLK), :] = jnp.zeros(
                (BLK, sel.shape[1]), BF16
            )
            return c

        lax.fori_loop(0, nnz, clear, 0)
        for e in range(nnz):
            dcat[:, e * BLK : (e + 1) * BLK] = d_ref[i, e]
        places = [(buf, j) for buf in bufs for j in range(buf.shape[0])]
        for q, (buf, j) in enumerate(places):
            e = row_at[i, q]

            @pl.when(e < nnz)
            def _():
                top = pl.multiple_of(e * BLK, BLK)

                def put(f, c):
                    g = col_at[i, q * nnz + f]
                    left = pl.multiple_of(g * BLK, BLK)
                    sel[pl.ds(top, BLK), pl.ds(left, BLK)] = buf[j, f]
                    return c

                lax.fori_loop(0, nnz, put, 0)

        def mult(n, c):
            at = pl.ds(pl.multiple_of(n * 256, 256), 256)
            out_ref[i, :, at] = jnp.dot(dcat[...], sel[:, at], preferred_element_type=F32)
            return c

        lax.fori_loop(0, width // 256, mult, 0)
        return carry

    lax.fori_loop(0, rows, one, 0)


def main_product(row_at, col_at, d, bufs):
    rows, nnz = d.shape[:2]
    return pl.pallas_call(
        main_kernel,
        out_shape=jax.ShapeDtypeStruct((rows, BLK, nnz * BLK), F32),
        in_specs=[SMEM, SMEM, VMEM] + [VMEM] * len(bufs),
        out_specs=VMEM,
        scratch_shapes=[
            pltpu.VMEM((nnz * BLK, (nnz + 1) * BLK), BF16),
            pltpu.VMEM((BLK, nnz * BLK), BF16),
        ],
        compiler_params=params(18),
        cost_estimate=cost(10, 10 << 20),
        name="hamiltonian",
    )(row_at, col_at, d, *bufs)


def final_kernel(at_ref, main_ref, d_ref, shift_ref, out_ref):
    rows, nnz = d_ref.shape[:2]
    for i in range(rows):
        for g in range(nnz):
            s = shift_ref[pl.ds(at_ref[i, g], 1), :]
            out_ref[i, g] = (
                main_ref[i, :, g * BLK : (g + 1) * BLK] + d_ref[i, g].astype(F32) * s
            ).astype(BF16)


def final(at, main, d, shift):
    return pl.pallas_call(
        final_kernel,
        out_shape=jax.ShapeDtypeStruct(d.shape, BF16),
        in_specs=[SMEM, VMEM, VMEM, VMEM],
        out_specs=VMEM,
        compiler_params=params(6),
        cost_estimate=cost(2, 4 << 20),
        name="final",
    )(at, main, d, shift)


ORDER = (0, 1, 3, 2)


def gather_hamiltonian(tiles, n_row):
    chips = n_row // 2
    assert chips == len(ORDER) and tiles.shape[0] == 2
    ahead = [(r, ((r // 2 + 1) % chips) * 2 + r % 2) for r in range(n_row)]
    behind = [(r, ((r // 2 - 1) % chips) * 2 + r % 2) for r in range(n_row)]
    one = lax.ppermute(tiles, "row", ahead)
    three = lax.ppermute(tiles, "row", behind)
    return one, three


def spread_hamiltonian(tiles, one, three, n_row):
    chips = n_row // 2
    ahead = [(r, ((r // 2 + 1) % chips) * 2 + r % 2) for r in range(n_row)]
    behind = [(r, ((r // 2 - 1) % chips) * 2 + r % 2) for r in range(n_row)]
    swap = [(r, r ^ 1) for r in range(n_row)]
    two_top = lax.ppermute(one[:1], "row", ahead)
    two_end = lax.ppermute(three[1:], "row", behind)
    same = [tiles, one, three, two_top, two_end]
    return same + [lax.ppermute(t, "row", swap) for t in same]


def positions(pattern, own_rows, n_row):
    me = lax.axis_index("row")
    chips = n_row // 2
    chip, core = me // 2, me % 2
    back = jnp.asarray(ORDER, jnp.int32)
    owner = (chip - back + chips) % chips * 2
    owner = jnp.concatenate([owner + core, owner + 1 - core])
    k = (owner[:, None] * own_rows + jnp.arange(own_rows, dtype=jnp.int32)).reshape(-1)
    own = lax.dynamic_slice_in_dim(pattern, me * own_rows, own_rows, 0)
    nnz = pattern.shape[1]
    local = own % (own_rows * n_row)
    index = jnp.arange(nnz, dtype=jnp.int32)
    row_at = jnp.min(
        jnp.where(local[:, None, :] == k[None, :, None], index, nnz), axis=2
    )
    rows = pattern[k]
    col_at = jnp.min(
        jnp.where(own[:, None, None, :] == rows[None, :, :, None], index, nnz), axis=3
    )
    shift_at = local // own_rows * 8 + local % own_rows
    return row_at, col_at.reshape(own_rows, -1), shift_at


def body(
    orbital_fragments,
    receiving_devices,
    fragment_grid_tile,
    outside_field_grid,
    density_matrix_tiles,
    energy_operator_tiles,
    tile_column_numbers,
):
    seg_dev = orbital_fragments.shape[0]
    n_orb = lax.axis_size("orb")
    n_row = lax.axis_size("row")
    devices = n_orb * n_row
    axes = ("orb", "row")

    def exchange(x, *block):
        pairs = x.reshape(devices, *block, LANES)
        got = lax.all_to_all(pairs, axes, split_axis=0, concat_axis=0, tiled=True)
        return got.reshape(-1, LANES)

    own_rows = density_matrix_tiles.shape[0]
    row_at, col_at, shift_at = positions(tile_column_numbers, own_rows, n_row)

    dest = receiving_devices.reshape(seg_dev // LANES, LANES)
    tile = fragment_grid_tile.reshape(seg_dev // LANES, LANES)
    me = (lax.axis_index("orb") * n_row + lax.axis_index("row")).reshape(1)
    outgoing, back = send_side(me, dest, tile, orbital_fragments, devices)
    outgoing, energy_operator_tiles = lax.optimization_barrier(
        (outgoing, energy_operator_tiles)
    )
    arrived = exchange(outgoing, PAIR // 2, 2)
    one, three = gather_hamiltonian(energy_operator_tiles, n_row)
    bufs = spread_hamiltonian(energy_operator_tiles, one, three, n_row)
    main = main_product(row_at, col_at, density_matrix_tiles, bufs)

    arrived, main = lax.optimization_barrier((arrived, main))
    results, charge = owner_step(arrived, outside_field_grid)
    applied, shift = unpack(back, exchange(results, CAP), orbital_fragments, n_row)
    shift = lax.all_to_all(shift, "row", split_axis=0, concat_axis=0, tiled=True)
    product = final(shift_at, main, density_matrix_tiles, shift.reshape(n_row * 8, LANES))
    return (applied, charge, product)


def solution(mesh):
    return jax.shard_map(
        body,
        mesh=mesh,
        in_specs=(
            P(("orb", "row"), None),
            P(("orb", "row"), None),
            P(("orb", "row")),
            P(("orb", "row"), None),
            P(("orb", "row"), None, None, None),
            P(("orb", "row"), None, None, None),
            P("orb", None),
        ),
        out_specs=(
            P(("orb", "row"), None),
            P(("orb", "row"), None),
            P(("orb", "row"), None, None, None),
        ),
        check_vma=False,
    )
```

```python
import functools

import jax
import jax.numpy as jnp
from jax import lax
from jax.experimental import pallas as pl
from jax.experimental.pallas import tpu as pltpu
from jax.sharding import PartitionSpec as P


BLK = 128
SEGF = 24
CAP = 48
PAIR = 50
LANES = 128
F32 = jnp.float32
BF16 = jnp.bfloat16
VMEM = pl.BlockSpec(memory_space=pltpu.VMEM)
SMEM = pl.BlockSpec(memory_space=pltpu.SMEM)


def params(mib):
    return pltpu.CompilerParams(vmem_limit_bytes=int(mib * 1024) << 10)


def cost(us, nbytes):
    return pl.CostEstimate(
        flops=int(us * 1e9), bytes_accessed=int(nbytes), transcendentals=0
    )


def iota(shape, axis):
    return lax.broadcasted_iota(jnp.int32, shape, axis)


def hot_rows(wide, which):
    return (wide == which).astype(F32).astype(BF16)


def columns(row):
    return jnp.transpose(jnp.broadcast_to(row, (LANES, LANES)))


ANY = pl.BlockSpec(memory_space=pltpu.HBM)


def widen(src_ref, dst):
    def step(i, c):
        at = pl.ds(pl.multiple_of(i * 256, 256), 256)
        dst[at, :] = src_ref[at, :].astype(F32)
        return c

    lax.fori_loop(0, src_ref.shape[0] // 256, step, 0)


STRIP = 8


def index_copies(slot_ref, regions, sems, strip):
    return [
        pltpu.make_async_copy(
            slot_ref.at[pl.ds(pl.multiple_of((strip + r) * STRIP, STRIP), STRIP)],
            region,
            sems.at[r],
        )
        for r, region in enumerate(regions)
    ]


def load_index(slot_ref, regions, sems, strip):
    for copy in index_copies(slot_ref, regions, sems, strip):
        copy.start()


def by_strips(slot_ref, regions, sems, work):
    strips = slot_ref.shape[0] // STRIP
    count = len(regions)

    def step(q, c):
        copies = index_copies(slot_ref, regions, sems, q * count)
        later = index_copies(slot_ref, regions, sems, (q + 1) * count)
        for r, region in enumerate(regions):
            copies[r].wait()
            first = pl.multiple_of((q * count + r) * STRIP * LANES, STRIP * LANES)
            work(first, lambda i: region[i // LANES, i % LANES])

            @pl.when((q + 1) * count < strips)
            def _():
                later[r].start()

        return c

    lax.fori_loop(0, strips // count, step, 0)


def send_kernel(
    devices,
    me_ref,
    dest_hbm,
    tile_hbm,
    x_hbm,
    out_hbm,
    back_ref,
    dest_ref,
    tile_ref,
    x_ref,
    run,
    rank,
    acc,
    slot_ref,
    smem0,
    smem1,
    xf,
    of,
    out_ref,
    sems,
    out_sems,
):
    loads = [
        pltpu.make_async_copy(src, dst, sems.at[i])
        for i, (src, dst) in enumerate(
            [(dest_hbm, dest_ref), (tile_hbm, tile_ref), (x_hbm, x_ref)]
        )
    ]
    for load in loads:
        load.start()
    blocks = dest_ref.shape[0]
    slots = of.shape[0]
    group = 12
    steps = blocks // group
    owner = iota((devices, LANES), 0)
    lane = iota((16, LANES), 1)
    src, dst = iota((LANES, LANES), 0), iota((LANES, LANES), 1)
    ahead = src < dst
    run[...] = jnp.zeros_like(run)
    loads[0].wait()

    def count(q, c):
        part = slots // steps
        of[pl.ds(pl.multiple_of(q * part, 128), part), :] = jnp.zeros((part, LANES), F32)
        hots, later = [], []
        for j in range(group):
            b = q * group + j
            d = dest_ref[pl.ds(b, 1), :]
            hots.append(hot_rows(owner, d))
            after = (lane > b).astype(F32).astype(BF16)
            later += [after] * (LANES // 16)
            same = (columns(d) == d) & ahead
            rank[pl.ds(b, 1), :] = jnp.sum(
                jnp.where(same, 1.0, 0.0), axis=0, keepdims=True
            )
        run[...] += jnp.dot(
            jnp.concatenate(hots, axis=1),
            jnp.concatenate(later, axis=0),
            preferred_element_type=F32,
        )
        return c

    lax.fori_loop(0, steps, count, 0)
    acc[:LANES, :] = jnp.concatenate(
        [jnp.transpose(run[i : i + LANES, :]) for i in range(0, devices, LANES)], axis=1
    )
    loads[1].wait()
    loads[2].wait()

    def order(q, c):
        part = group * LANES
        rows = pl.ds(pl.multiple_of(q * part, part), part)
        xf[rows, :] = x_ref[rows, :].astype(F32)
        for j in range(group):
            b = q * group + j
            d = dest_ref[pl.ds(b, 1), :]
            table = jnp.broadcast_to(acc[pl.ds(b, 1), :], (16, devices)).astype(BF16)
            before = jnp.dot(table, hot_rows(owner, d), preferred_element_type=F32)
            mine = (before[0:1] + rank[pl.ds(b, 1), :]).astype(jnp.int32)
            rank[pl.ds(b, 1), :] = mine.astype(F32)
            slot_ref[pl.ds(b, 1), :] = d * PAIR + mine
            back_ref[pl.ds(b, 1), :] = d * CAP + mine
        return c

    lax.fori_loop(0, steps, order, 0)
    regions = (smem0, smem1)
    index_sems = sems.at[pl.ds(3, 2)]
    load_index(slot_ref, regions, index_sems, 0)
    turn = me_ref[0] * PAIR
    acc[...] = jnp.zeros_like(acc)
    few = 4

    def mark(first):
        hots, spreads = [], []
        for j in range(few):
            b = first + j
            hots.append(hot_rows(owner, dest_ref[pl.ds(b, 1), :]))
            place = rank[pl.ds(b, 1), :].astype(jnp.int32) + turn
            at = src == (place & (LANES - 1))
            label = tile_ref[pl.ds(b, 1), :] + 1
            high = jnp.where(at, (label >> 2).astype(F32), 0.0)
            low = jnp.where(at, (label & 3).astype(F32), 0.0)
            spreads.append(jnp.concatenate([high, low], axis=0).astype(BF16))
        acc[...] += lax.dot_general(
            jnp.concatenate(hots, axis=1),
            jnp.concatenate(spreads, axis=1),
            (((1,), (1,)), ((), ())),
            preferred_element_type=F32,
        )

    def move(first, place):
        here = xf.at[pl.ds(first, STRIP * LANES)]
        block = first // LANES
        for q in range(STRIP // few):
            mark(block + q * few)
            for i in range(q * few * LANES, (q + 1) * few * LANES):
                of[pl.ds(place(i), 1), :] = here[i : i + 1, :]

    by_strips(slot_ref, regions, index_sems, move)
    of[pl.ds(CAP, devices, stride=PAIR), :] = acc[:, :LANES]
    of[pl.ds(CAP + 1, devices, stride=PAIR), :] = acc[:, LANES:]
    for copy in put_out(lambda at: of[at, :], out_ref, out_hbm, out_sems, 320):
        copy.wait()


def put_out(get, out_ref, out_hbm, sems, size):
    pieces = sems.shape[0]
    part = out_ref.shape[0] // pieces
    copies = []
    for p in range(pieces):

        def narrow(i, c):
            at = pl.ds(pl.multiple_of(p * part + i * size, size), size)
            out_ref[at, :] = get(at).astype(BF16)
            return c

        lax.fori_loop(0, part // size, narrow, 0)
        at = pl.ds(p * part, part)
        copies.append(
            pltpu.make_async_copy(out_ref.at[at], out_hbm.at[at], sems.at[p])
        )
        copies[-1].start()
    return copies


def send_side(me, dest, tile, x, devices):
    blocks = dest.shape[0]
    slots = devices * PAIR
    return pl.pallas_call(
        functools.partial(send_kernel, devices),
        out_shape=(
            jax.ShapeDtypeStruct((slots, LANES), BF16),
            jax.ShapeDtypeStruct((blocks, LANES), jnp.int32),
        ),
        in_specs=[SMEM, ANY, ANY, ANY],
        out_specs=(ANY, VMEM),
        scratch_shapes=[
            pltpu.VMEM((blocks, LANES), jnp.int32),
            pltpu.VMEM((blocks, LANES), jnp.int32),
            pltpu.VMEM(x.shape, BF16),
            pltpu.VMEM((devices, LANES), F32),
            pltpu.VMEM((blocks, LANES), F32),
            pltpu.VMEM((devices, 2 * LANES), F32),
            pltpu.VMEM((blocks, LANES), jnp.int32),
            pltpu.SMEM((STRIP, LANES), jnp.int32),
            pltpu.SMEM((STRIP, LANES), jnp.int32),
            pltpu.VMEM(x.shape, F32),
            pltpu.VMEM((slots, LANES), F32),
            pltpu.VMEM((slots, LANES), BF16),
            pltpu.SemaphoreType.DMA((5,)),
            pltpu.SemaphoreType.DMA((5,)),
        ],
        compiler_params=params(61),
        cost_estimate=cost(12, 5 << 20),
        name="send",
    )(me, dest, tile, x)


OWNER = 28
DEPTH = 1280
CHUNK = 1280


def slot_labels(high, low):
    devices = high.shape[0]
    groups = -(-devices * PAIR // LANES // 8) * 8
    source, lane = iota((devices, LANES), 0), iota((devices, LANES), 1)
    offset = (source * PAIR) & (LANES - 1)
    near = lane >= offset
    k, s = iota((groups, devices), 0), iota((groups, devices), 1)
    first = (s * PAIR) >> 7
    left = jnp.concatenate([first == k, first + 1 == k], axis=1)
    left = left.astype(F32).astype(BF16)

    def part(x):
        return jnp.concatenate(
            [jnp.where(near, x, 0.0), jnp.where(near, 0.0, x)], axis=0
        ).astype(BF16)

    right = jnp.concatenate([part(high), part(low)], axis=1)
    both = jnp.dot(left, right, preferred_element_type=F32)
    return (both[:, :LANES] * 4.0 + both[:, LANES:]).astype(jnp.int32) - 1


def owner_kernel(
    v_ref,
    field_hbm,
    out_ref,
    charge_ref,
    vf,
    label,
    acc,
    pot,
    field_ref,
    sem,
):
    slots = v_ref.shape[0]
    tiles = charge_ref.shape[0]
    devices = slots // PAIR
    fetch = pltpu.make_async_copy(field_hbm, field_ref, sem)
    fetch.start()
    acc[...] = jnp.zeros_like(acc)
    widen(v_ref, vf)
    label[...] = slot_labels(
        vf[pl.ds(CAP, devices, stride=PAIR), :],
        vf[pl.ds(CAP + 1, devices, stride=PAIR), :],
    )
    cell = iota((tiles, LANES), 0)

    def add(k, c):
        hot = []
        for j in range(DEPTH // LANES):
            hot.append(hot_rows(cell, label[pl.ds(k * (DEPTH // LANES) + j, 1), :]))
        v = vf[pl.ds(pl.multiple_of(k * DEPTH, DEPTH), DEPTH), :]
        square = v * v
        high = square.astype(BF16)
        low = (square - high.astype(F32)).astype(BF16)
        acc[...] += jnp.dot(
            jnp.concatenate(hot, axis=1),
            jnp.concatenate([high, low], axis=1),
            preferred_element_type=F32,
        )
        return c

    lax.fori_loop(0, slots // DEPTH, add, 0)
    charge = acc[:, :LANES] + acc[:, LANES:]
    charge_ref[...] = charge
    fetch.wait()
    field = field_ref[...] - 1.5 * jnp.exp(jnp.log(1.0 + charge) * (1.0 / 3.0))
    high = field.astype(BF16)
    pot[:, :LANES] = high
    pot[:, LANES:] = (field - high.astype(F32)).astype(BF16)
    lane = iota((LANES, tiles), 1)

    def apply(k, c):
        hot = []
        for j in range(CHUNK // LANES):
            col = columns(label[pl.ds(k * (CHUNK // LANES) + j, 1), :])
            hot.append(hot_rows(lane, jnp.concatenate([col] * (tiles // LANES), axis=1)))
        got = jnp.dot(
            jnp.concatenate(hot, axis=0), pot[...], preferred_element_type=F32
        )
        at = pl.ds(pl.multiple_of(k * CHUNK, CHUNK), CHUNK)
        here = got[:, :LANES] + got[:, LANES:]
        vf[at, :] = here * vf[at, :]
        return c

    lax.fori_loop(0, slots // CHUNK, apply, 0)
    pairs = 8

    def narrow(i, c):
        source = vf.at[pl.ds(pl.multiple_of(i * pairs * PAIR, 8), pairs * PAIR)]
        at = pl.ds(pl.multiple_of(i * pairs * CAP, pairs * CAP), pairs * CAP)
        out_ref[at, :] = jnp.concatenate(
            [source[j * PAIR : j * PAIR + CAP, :] for j in range(pairs)], axis=0
        ).astype(BF16)
        return c

    lax.fori_loop(0, devices // pairs, narrow, 0)


def owner_step(v, field):
    slots = v.shape[0]
    tiles = field.shape[0]
    return pl.pallas_call(
        owner_kernel,
        out_shape=(
            jax.ShapeDtypeStruct((slots // PAIR * CAP, LANES), BF16),
            jax.ShapeDtypeStruct((tiles, LANES), F32),
        ),
        in_specs=[VMEM, ANY],
        out_specs=(VMEM, VMEM),
        scratch_shapes=[
            pltpu.VMEM((slots, LANES), F32),
            pltpu.VMEM((-(-slots // LANES // 8) * 8, LANES), jnp.int32),
            pltpu.VMEM((tiles, 2 * LANES), F32),
            pltpu.VMEM((tiles, 2 * LANES), BF16),
            pltpu.VMEM((tiles, LANES), F32),
            pltpu.SemaphoreType.DMA,
        ],
        compiler_params=params(OWNER),
        cost_estimate=cost(16, 7 << 20),
        name="owner",
    )(v, field)


def unpack_kernel(
    n_row,
    slot_ref,
    ret_ref,
    x_ref,
    out_hbm,
    shift_ref,
    rf,
    of,
    part,
    out_ref,
    smem0,
    smem1,
    sems,
    out_sems,
):
    rows = x_ref.shape[0]
    regions = (smem0, smem1)
    load_index(slot_ref, regions, sems, 0)
    widen(ret_ref, rf)

    def take(first, place):
        rows_out = of.at[pl.ds(first, STRIP * LANES)]
        for i in range(STRIP * LANES):
            rows_out[i : i + 1, :] = rf[pl.ds(place(i), 1), :]

    by_strips(slot_ref, regions, sems, take)
    count = 8

    def with_shift(at):
        got = of[at, :]
        work = (got * x_ref[at, :].astype(F32)).reshape(count, SEGF, LANES)
        first = pl.multiple_of(at.start // SEGF, count)
        part[pl.ds(first, count), :] = jnp.sum(work, axis=1)
        return got

    copies = put_out(with_shift, out_ref, out_hbm, out_sems, count * SEGF)
    functions = rows // SEGF
    total = lax.dot_general(
        jnp.ones((8, LANES), F32),
        part[...],
        (((1,), (1,)), ((), ())),
        precision=lax.Precision.HIGHEST,
        preferred_element_type=F32,
    )
    total = total * (1.0 / (SEGF * LANES))
    one = jnp.concatenate(
        [total[0:1, i * BLK : (i + 1) * BLK] for i in range(functions // BLK)]
        + [jnp.zeros((8 - functions // BLK, BLK), F32)],
        axis=0,
    )
    one = one.astype(BF16).astype(F32)
    for r in range(n_row):
        shift_ref[r] = one
    for copy in copies:
        copy.wait()


def unpack(slot, ret, x, n_row):
    rows = x.shape[0]
    return pl.pallas_call(
        functools.partial(unpack_kernel, n_row),
        out_shape=(
            jax.ShapeDtypeStruct((rows, LANES), BF16),
            jax.ShapeDtypeStruct((n_row, 8, LANES), F32),
        ),
        in_specs=[VMEM, VMEM, VMEM],
        out_specs=(ANY, VMEM),
        scratch_shapes=[
            pltpu.VMEM(ret.shape, F32),
            pltpu.VMEM((rows, LANES), F32),
            pltpu.VMEM((rows // SEGF, LANES), F32),
            pltpu.VMEM((rows, LANES), BF16),
            pltpu.SMEM((STRIP, LANES), jnp.int32),
            pltpu.SMEM((STRIP, LANES), jnp.int32),
            pltpu.SemaphoreType.DMA((2,)),
            pltpu.SemaphoreType.DMA((4,)),
        ],
        compiler_params=params(20),
        cost_estimate=cost(10, 7 << 20),
        name="unpack",
    )(slot, ret, x)


def main_kernel(row_at, col_at, d_ref, *refs):
    bufs, (out_ref, sel, dcat) = refs[:-3], refs[-3:]
    rows, nnz = d_ref.shape[:2]
    width = nnz * BLK

    def one(i, carry):
        def clear(e, c):
            sel[pl.ds(pl.multiple_of(e * BLK, BLK), BLK), :] = jnp.zeros(
                (BLK, sel.shape[1]), BF16
            )
            return c

        lax.fori_loop(0, nnz, clear, 0)
        for e in range(nnz):
            dcat[:, e * BLK : (e + 1) * BLK] = d_ref[i, e]
        places = [(buf, j) for buf in bufs for j in range(buf.shape[0])]
        for q, (buf, j) in enumerate(places):
            e = row_at[i, q]

            @pl.when(e < nnz)
            def _():
                top = pl.multiple_of(e * BLK, BLK)

                def put(f, c):
                    g = col_at[i, q * nnz + f]
                    left = pl.multiple_of(g * BLK, BLK)
                    sel[pl.ds(top, BLK), pl.ds(left, BLK)] = buf[j, f]
                    return c

                lax.fori_loop(0, nnz, put, 0)

        def mult(n, c):
            at = pl.ds(pl.multiple_of(n * 256, 256), 256)
            out_ref[i, :, at] = jnp.dot(dcat[...], sel[:, at], preferred_element_type=F32)
            return c

        lax.fori_loop(0, width // 256, mult, 0)
        return carry

    lax.fori_loop(0, rows, one, 0)


def main_product(row_at, col_at, d, bufs):
    rows, nnz = d.shape[:2]
    return pl.pallas_call(
        main_kernel,
        out_shape=jax.ShapeDtypeStruct((rows, BLK, nnz * BLK), F32),
        in_specs=[SMEM, SMEM, VMEM] + [VMEM] * len(bufs),
        out_specs=VMEM,
        scratch_shapes=[
            pltpu.VMEM((nnz * BLK, (nnz + 1) * BLK), BF16),
            pltpu.VMEM((BLK, nnz * BLK), BF16),
        ],
        compiler_params=params(18),
        cost_estimate=cost(10, 10 << 20),
        name="hamiltonian",
    )(row_at, col_at, d, *bufs)


def final_kernel(at_ref, main_ref, d_ref, shift_ref, out_ref):
    rows, nnz = d_ref.shape[:2]
    for i in range(rows):
        for g in range(nnz):
            s = shift_ref[pl.ds(at_ref[i, g], 1), :]
            out_ref[i, g] = (
                main_ref[i, :, g * BLK : (g + 1) * BLK] + d_ref[i, g].astype(F32) * s
            ).astype(BF16)


def final(at, main, d, shift):
    return pl.pallas_call(
        final_kernel,
        out_shape=jax.ShapeDtypeStruct(d.shape, BF16),
        in_specs=[SMEM, VMEM, VMEM, VMEM],
        out_specs=VMEM,
        compiler_params=params(6),
        cost_estimate=cost(2, 4 << 20),
        name="final",
    )(at, main, d, shift)


ORDER = (0, 1, 3, 2)


def gather_hamiltonian(tiles, n_row):
    chips = n_row // 2
    assert chips == len(ORDER) and tiles.shape[0] == 2
    ahead = [(r, ((r // 2 + 1) % chips) * 2 + r % 2) for r in range(n_row)]
    behind = [(r, ((r // 2 - 1) % chips) * 2 + r % 2) for r in range(n_row)]
    one = lax.ppermute(tiles, "row", ahead)
    three = lax.ppermute(tiles, "row", behind)
    return one, three


def spread_hamiltonian(tiles, one, three, n_row):
    chips = n_row // 2
    ahead = [(r, ((r // 2 + 1) % chips) * 2 + r % 2) for r in range(n_row)]
    behind = [(r, ((r // 2 - 1) % chips) * 2 + r % 2) for r in range(n_row)]
    swap = [(r, r ^ 1) for r in range(n_row)]
    two_top = lax.ppermute(one[:1], "row", ahead)
    two_end = lax.ppermute(three[1:], "row", behind)
    same = [tiles, one, three, two_top, two_end]
    return same + [lax.ppermute(t, "row", swap) for t in same]


def positions(pattern, own_rows, n_row):
    me = lax.axis_index("row")
    chips = n_row // 2
    chip, core = me // 2, me % 2
    back = jnp.asarray(ORDER, jnp.int32)
    owner = (chip - back + chips) % chips * 2
    owner = jnp.concatenate([owner + core, owner + 1 - core])
    k = (owner[:, None] * own_rows + jnp.arange(own_rows, dtype=jnp.int32)).reshape(-1)
    own = lax.dynamic_slice_in_dim(pattern, me * own_rows, own_rows, 0)
    nnz = pattern.shape[1]
    local = own % (own_rows * n_row)
    index = jnp.arange(nnz, dtype=jnp.int32)
    row_at = jnp.min(
        jnp.where(local[:, None, :] == k[None, :, None], index, nnz), axis=2
    )
    rows = pattern[k]
    col_at = jnp.min(
        jnp.where(own[:, None, None, :] == rows[None, :, :, None], index, nnz), axis=3
    )
    shift_at = local // own_rows * 8 + local % own_rows
    return row_at, col_at.reshape(own_rows, -1), shift_at


def body(
    orbital_fragments,
    receiving_devices,
    fragment_grid_tile,
    outside_field_grid,
    density_matrix_tiles,
    energy_operator_tiles,
    tile_column_numbers,
):
    seg_dev = orbital_fragments.shape[0]
    n_orb = lax.axis_size("orb")
    n_row = lax.axis_size("row")
    devices = n_orb * n_row
    axes = ("orb", "row")

    def exchange(x, *block):
        pairs = x.reshape(devices, *block, LANES)
        got = lax.all_to_all(pairs, axes, split_axis=0, concat_axis=0, tiled=True)
        return got.reshape(-1, LANES)

    own_rows = density_matrix_tiles.shape[0]
    row_at, col_at, shift_at = positions(tile_column_numbers, own_rows, n_row)
    one, three = gather_hamiltonian(energy_operator_tiles, n_row)

    dest = receiving_devices.reshape(seg_dev // LANES, LANES)
    tile = fragment_grid_tile.reshape(seg_dev // LANES, LANES)
    me = (lax.axis_index("orb") * n_row + lax.axis_index("row")).reshape(1)
    outgoing, back = send_side(me, dest, tile, orbital_fragments, devices)
    arrived = exchange(outgoing, PAIR // 2, 2)
    bufs = spread_hamiltonian(energy_operator_tiles, one, three, n_row)
    main = main_product(row_at, col_at, density_matrix_tiles, bufs)

    arrived, main = lax.optimization_barrier((arrived, main))
    results, charge = owner_step(arrived, outside_field_grid)
    applied, shift = unpack(back, exchange(results, CAP), orbital_fragments, n_row)
    shift = lax.all_to_all(shift, "row", split_axis=0, concat_axis=0, tiled=True)
    product = final(shift_at, main, density_matrix_tiles, shift.reshape(n_row * 8, LANES))
    return (applied, charge, product)


def solution(mesh):
    return jax.shard_map(
        body,
        mesh=mesh,
        in_specs=(
            P(("orb", "row"), None),
            P(("orb", "row"), None),
            P(("orb", "row")),
            P(("orb", "row"), None),
            P(("orb", "row"), None, None, None),
            P(("orb", "row"), None, None, None),
            P("orb", None),
        ),
        out_specs=(
            P(("orb", "row"), None),
            P(("orb", "row"), None),
            P(("orb", "row"), None, None, None),
        ),
        check_vma=False,
    )
```

```python
import functools

import jax
import jax.numpy as jnp
from jax import lax
from jax.experimental import pallas as pl
from jax.experimental.pallas import tpu as pltpu
from jax.sharding import PartitionSpec as P


BLK = 128
SEGF = 24
CAP = 48
PAIR = 50
LANES = 128
F32 = jnp.float32
BF16 = jnp.bfloat16
VMEM = pl.BlockSpec(memory_space=pltpu.VMEM)
SMEM = pl.BlockSpec(memory_space=pltpu.SMEM)


def params(mib):
    return pltpu.CompilerParams(vmem_limit_bytes=int(mib * 1024) << 10)


def cost(us, nbytes):
    return pl.CostEstimate(
        flops=int(us * 1e9), bytes_accessed=int(nbytes), transcendentals=0
    )


def iota(shape, axis):
    return lax.broadcasted_iota(jnp.int32, shape, axis)


def hot_rows(wide, which):
    return (wide == which).astype(F32).astype(BF16)


def columns(row):
    return jnp.transpose(jnp.broadcast_to(row, (LANES, LANES)))


ANY = pl.BlockSpec(memory_space=pltpu.HBM)


def widen(src_ref, dst):
    def step(i, c):
        at = pl.ds(pl.multiple_of(i * 256, 256), 256)
        dst[at, :] = src_ref[at, :].astype(F32)
        return c

    lax.fori_loop(0, src_ref.shape[0] // 256, step, 0)


STRIP = 8
GROUP = 16


def index_copies(slot_ref, regions, sems, strip):
    return [
        pltpu.make_async_copy(
            slot_ref.at[pl.ds(pl.multiple_of((strip + r) * STRIP, STRIP), STRIP)],
            region,
            sems.at[r],
        )
        for r, region in enumerate(regions)
    ]


def load_index(slot_ref, regions, sems, strip):
    for copy in index_copies(slot_ref, regions, sems, strip):
        copy.start()


def by_strips(slot_ref, regions, sems, work):
    strips = slot_ref.shape[0] // STRIP
    count = len(regions)

    def step(q, c):
        copies = index_copies(slot_ref, regions, sems, q * count)
        later = index_copies(slot_ref, regions, sems, (q + 1) * count)
        for r, region in enumerate(regions):
            copies[r].wait()
            first = pl.multiple_of((q * count + r) * STRIP * LANES, STRIP * LANES)
            work(first, lambda i: region[i // LANES, i % LANES])

            @pl.when((q + 1) * count < strips)
            def _():
                later[r].start()

        return c

    lax.fori_loop(0, strips // count, step, 0)


def send_kernel(
    devices,
    me_ref,
    dest_hbm,
    tile_hbm,
    x_hbm,
    out_hbm,
    back_ref,
    dest_ref,
    tile_ref,
    x_ref,
    run,
    rank,
    acc,
    slot_ref,
    smem0,
    smem1,
    smem2,
    xf,
    of,
    out_ref,
    sems,
    out_sems,
):
    loads = [
        pltpu.make_async_copy(src, dst, sems.at[i])
        for i, (src, dst) in enumerate(
            [(dest_hbm, dest_ref), (tile_hbm, tile_ref), (x_hbm, x_ref)]
        )
    ]
    for load in loads:
        load.start()
    blocks = dest_ref.shape[0]
    slots = of.shape[0]
    group = GROUP
    steps = blocks // group
    owner = iota((devices, LANES), 0)
    lane = iota((16, LANES), 1)
    src, dst = iota((LANES, LANES), 0), iota((LANES, LANES), 1)
    ahead = src < dst
    run[...] = jnp.zeros_like(run)
    loads[0].wait()

    def count(q, c):
        part = slots // steps
        of[pl.ds(pl.multiple_of(q * part, 128), part), :] = jnp.zeros((part, LANES), F32)
        hots, later = [], []
        for j in range(group):
            b = q * group + j
            d = dest_ref[pl.ds(b, 1), :]
            hots.append(hot_rows(owner, d))
            after = (lane > b).astype(F32).astype(BF16)
            later += [after] * (LANES // 16)
            same = (columns(d) == d) & ahead
            rank[pl.ds(b, 1), :] = jnp.sum(
                jnp.where(same, 1.0, 0.0), axis=0, keepdims=True
            )
        run[...] += jnp.dot(
            jnp.concatenate(hots, axis=1),
            jnp.concatenate(later, axis=0),
            preferred_element_type=F32,
        )
        return c

    lax.fori_loop(0, steps, count, 0)
    acc[:LANES, :] = jnp.concatenate(
        [jnp.transpose(run[i : i + LANES, :]) for i in range(0, devices, LANES)], axis=1
    )
    loads[1].wait()
    loads[2].wait()

    def order(q, c):
        part = group * LANES
        rows = pl.ds(pl.multiple_of(q * part, part), part)
        xf[rows, :] = x_ref[rows, :].astype(F32)
        for j in range(group):
            b = q * group + j
            d = dest_ref[pl.ds(b, 1), :]
            table = jnp.broadcast_to(acc[pl.ds(b, 1), :], (16, devices)).astype(BF16)
            before = jnp.dot(table, hot_rows(owner, d), preferred_element_type=F32)
            mine = (before[0:1] + rank[pl.ds(b, 1), :]).astype(jnp.int32)
            rank[pl.ds(b, 1), :] = mine.astype(F32)
            slot_ref[pl.ds(b, 1), :] = d * PAIR + mine
            back_ref[pl.ds(b, 1), :] = d * CAP + mine
        return c

    lax.fori_loop(0, steps, order, 0)
    regions = (smem0, smem1, smem2)
    index_sems = sems.at[pl.ds(3, 3)]
    load_index(slot_ref, regions, index_sems, 0)
    turn = me_ref[0] * PAIR
    acc[...] = jnp.zeros_like(acc)
    few = 4

    def mark(first):
        hots, spreads = [], []
        for j in range(few):
            b = first + j
            hots.append(hot_rows(owner, dest_ref[pl.ds(b, 1), :]))
            place = rank[pl.ds(b, 1), :].astype(jnp.int32) + turn
            at = src == (place & (LANES - 1))
            label = tile_ref[pl.ds(b, 1), :] + 1
            high = jnp.where(at, (label >> 2).astype(F32), 0.0)
            low = jnp.where(at, (label & 3).astype(F32), 0.0)
            spreads.append(jnp.concatenate([high, low], axis=0).astype(BF16))
        acc[...] += lax.dot_general(
            jnp.concatenate(hots, axis=1),
            jnp.concatenate(spreads, axis=1),
            (((1,), (1,)), ((), ())),
            preferred_element_type=F32,
        )

    def move(first, place):
        here = xf.at[pl.ds(first, STRIP * LANES)]
        block = first // LANES
        for q in range(STRIP // few):
            mark(block + q * few)
            for i in range(q * few * LANES, (q + 1) * few * LANES):
                of[pl.ds(place(i), 1), :] = here[i : i + 1, :]

    by_strips(slot_ref, regions, index_sems, move)
    of[pl.ds(CAP, devices, stride=PAIR), :] = acc[:, :LANES]
    of[pl.ds(CAP + 1, devices, stride=PAIR), :] = acc[:, LANES:]
    for copy in put_out(lambda at: of[at, :], out_ref, out_hbm, out_sems, 320):
        copy.wait()


def put_out(get, out_ref, out_hbm, sems, size):
    pieces = sems.shape[0]
    part = out_ref.shape[0] // pieces
    copies = []
    for p in range(pieces):

        def narrow(i, c):
            at = pl.ds(pl.multiple_of(p * part + i * size, size), size)
            out_ref[at, :] = get(at).astype(BF16)
            return c

        lax.fori_loop(0, part // size, narrow, 0)
        at = pl.ds(p * part, part)
        copies.append(
            pltpu.make_async_copy(out_ref.at[at], out_hbm.at[at], sems.at[p])
        )
        copies[-1].start()
    return copies


def send_side(me, dest, tile, x, devices):
    blocks = dest.shape[0]
    slots = devices * PAIR
    return pl.pallas_call(
        functools.partial(send_kernel, devices),
        out_shape=(
            jax.ShapeDtypeStruct((slots, LANES), BF16),
            jax.ShapeDtypeStruct((blocks, LANES), jnp.int32),
        ),
        in_specs=[SMEM, ANY, ANY, ANY],
        out_specs=(ANY, VMEM),
        scratch_shapes=[
            pltpu.VMEM((blocks, LANES), jnp.int32),
            pltpu.VMEM((blocks, LANES), jnp.int32),
            pltpu.VMEM(x.shape, BF16),
            pltpu.VMEM((devices, LANES), F32),
            pltpu.VMEM((blocks, LANES), F32),
            pltpu.VMEM((devices, 2 * LANES), F32),
            pltpu.VMEM((blocks, LANES), jnp.int32),
            pltpu.SMEM((STRIP, LANES), jnp.int32),
            pltpu.SMEM((STRIP, LANES), jnp.int32),
            pltpu.SMEM((STRIP, LANES), jnp.int32),
            pltpu.VMEM(x.shape, F32),
            pltpu.VMEM((slots, LANES), F32),
            pltpu.VMEM((slots, LANES), BF16),
            pltpu.SemaphoreType.DMA((6,)),
            pltpu.SemaphoreType.DMA((5,)),
        ],
        compiler_params=params(61),
        cost_estimate=cost(12, 5 << 20),
        name="send",
    )(me, dest, tile, x)


OWNER = 28
DEPTH = 1280
CHUNK = 1280


def slot_labels(high, low):
    devices = high.shape[0]
    groups = -(-devices * PAIR // LANES // 8) * 8
    source, lane = iota((devices, LANES), 0), iota((devices, LANES), 1)
    offset = (source * PAIR) & (LANES - 1)
    near = lane >= offset
    k, s = iota((groups, devices), 0), iota((groups, devices), 1)
    first = (s * PAIR) >> 7
    left = jnp.concatenate([first == k, first + 1 == k], axis=1)
    left = left.astype(F32).astype(BF16)

    def part(x):
        return jnp.concatenate(
            [jnp.where(near, x, 0.0), jnp.where(near, 0.0, x)], axis=0
        ).astype(BF16)

    right = jnp.concatenate([part(high), part(low)], axis=1)
    both = jnp.dot(left, right, preferred_element_type=F32)
    return (both[:, :LANES] * 4.0 + both[:, LANES:]).astype(jnp.int32) - 1


def owner_kernel(
    v_ref,
    field_hbm,
    out_ref,
    charge_ref,
    vf,
    label,
    acc,
    pot,
    field_ref,
    sem,
):
    slots = v_ref.shape[0]
    tiles = charge_ref.shape[0]
    devices = slots // PAIR
    fetch = pltpu.make_async_copy(field_hbm, field_ref, sem)
    fetch.start()
    acc[...] = jnp.zeros_like(acc)
    widen(v_ref, vf)
    label[...] = slot_labels(
        vf[pl.ds(CAP, devices, stride=PAIR), :],
        vf[pl.ds(CAP + 1, devices, stride=PAIR), :],
    )
    cell = iota((tiles, LANES), 0)

    def add(k, c):
        hot = []
        for j in range(DEPTH // LANES):
            hot.append(hot_rows(cell, label[pl.ds(k * (DEPTH // LANES) + j, 1), :]))
        v = vf[pl.ds(pl.multiple_of(k * DEPTH, DEPTH), DEPTH), :]
        square = v * v
        high = square.astype(BF16)
        low = (square - high.astype(F32)).astype(BF16)
        acc[...] += jnp.dot(
            jnp.concatenate(hot, axis=1),
            jnp.concatenate([high, low], axis=1),
            preferred_element_type=F32,
        )
        return c

    lax.fori_loop(0, slots // DEPTH, add, 0)
    charge = acc[:, :LANES] + acc[:, LANES:]
    charge_ref[...] = charge
    fetch.wait()
    field = field_ref[...] - 1.5 * jnp.exp(jnp.log(1.0 + charge) * (1.0 / 3.0))
    high = field.astype(BF16)
    pot[:, :LANES] = high
    pot[:, LANES:] = (field - high.astype(F32)).astype(BF16)
    lane = iota((LANES, tiles), 1)

    def apply(k, c):
        hot = []
        for j in range(CHUNK // LANES):
            col = columns(label[pl.ds(k * (CHUNK // LANES) + j, 1), :])
            hot.append(hot_rows(lane, jnp.concatenate([col] * (tiles // LANES), axis=1)))
        got = jnp.dot(
            jnp.concatenate(hot, axis=0), pot[...], preferred_element_type=F32
        )
        at = pl.ds(pl.multiple_of(k * CHUNK, CHUNK), CHUNK)
        here = got[:, :LANES] + got[:, LANES:]
        vf[at, :] = here * vf[at, :]
        return c

    lax.fori_loop(0, slots // CHUNK, apply, 0)
    pairs = 8

    def narrow(i, c):
        source = vf.at[pl.ds(pl.multiple_of(i * pairs * PAIR, 8), pairs * PAIR)]
        at = pl.ds(pl.multiple_of(i * pairs * CAP, pairs * CAP), pairs * CAP)
        out_ref[at, :] = jnp.concatenate(
            [source[j * PAIR : j * PAIR + CAP, :] for j in range(pairs)], axis=0
        ).astype(BF16)
        return c

    lax.fori_loop(0, devices // pairs, narrow, 0)


def owner_step(v, field):
    slots = v.shape[0]
    tiles = field.shape[0]
    return pl.pallas_call(
        owner_kernel,
        out_shape=(
            jax.ShapeDtypeStruct((slots // PAIR * CAP, LANES), BF16),
            jax.ShapeDtypeStruct((tiles, LANES), F32),
        ),
        in_specs=[VMEM, ANY],
        out_specs=(VMEM, VMEM),
        scratch_shapes=[
            pltpu.VMEM((slots, LANES), F32),
            pltpu.VMEM((-(-slots // LANES // 8) * 8, LANES), jnp.int32),
            pltpu.VMEM((tiles, 2 * LANES), F32),
            pltpu.VMEM((tiles, 2 * LANES), BF16),
            pltpu.VMEM((tiles, LANES), F32),
            pltpu.SemaphoreType.DMA,
        ],
        compiler_params=params(OWNER),
        cost_estimate=cost(16, 7 << 20),
        name="owner",
    )(v, field)


def unpack_kernel(
    n_row,
    slot_ref,
    ret_ref,
    x_ref,
    out_hbm,
    shift_ref,
    rf,
    of,
    part,
    out_ref,
    smem0,
    smem1,
    smem2,
    sems,
    out_sems,
):
    rows = x_ref.shape[0]
    regions = (smem0, smem1, smem2)
    load_index(slot_ref, regions, sems, 0)
    widen(ret_ref, rf)

    def take(first, place):
        rows_out = of.at[pl.ds(first, STRIP * LANES)]
        for i in range(STRIP * LANES):
            rows_out[i : i + 1, :] = rf[pl.ds(place(i), 1), :]

    by_strips(slot_ref, regions, sems, take)
    count = 8

    def with_shift(at):
        got = of[at, :]
        work = (got * x_ref[at, :].astype(F32)).reshape(count, SEGF, LANES)
        first = pl.multiple_of(at.start // SEGF, count)
        part[pl.ds(first, count), :] = jnp.sum(work, axis=1)
        return got

    copies = put_out(with_shift, out_ref, out_hbm, out_sems, count * SEGF)
    functions = rows // SEGF
    total = lax.dot_general(
        jnp.ones((8, LANES), F32),
        part[...],
        (((1,), (1,)), ((), ())),
        precision=lax.Precision.HIGHEST,
        preferred_element_type=F32,
    )
    total = total * (1.0 / (SEGF * LANES))
    one = jnp.concatenate(
        [total[0:1, i * BLK : (i + 1) * BLK] for i in range(functions // BLK)]
        + [jnp.zeros((8 - functions // BLK, BLK), F32)],
        axis=0,
    )
    one = one.astype(BF16).astype(F32)
    for r in range(n_row):
        shift_ref[r] = one
    for copy in copies:
        copy.wait()


def unpack(slot, ret, x, n_row):
    rows = x.shape[0]
    return pl.pallas_call(
        functools.partial(unpack_kernel, n_row),
        out_shape=(
            jax.ShapeDtypeStruct((rows, LANES), BF16),
            jax.ShapeDtypeStruct((n_row, 8, LANES), F32),
        ),
        in_specs=[VMEM, VMEM, VMEM],
        out_specs=(ANY, VMEM),
        scratch_shapes=[
            pltpu.VMEM(ret.shape, F32),
            pltpu.VMEM((rows, LANES), F32),
            pltpu.VMEM((rows // SEGF, LANES), F32),
            pltpu.VMEM((rows, LANES), BF16),
            pltpu.SMEM((STRIP, LANES), jnp.int32),
            pltpu.SMEM((STRIP, LANES), jnp.int32),
            pltpu.SMEM((STRIP, LANES), jnp.int32),
            pltpu.SemaphoreType.DMA((3,)),
            pltpu.SemaphoreType.DMA((4,)),
        ],
        compiler_params=params(20),
        cost_estimate=cost(10, 7 << 20),
        name="unpack",
    )(slot, ret, x)


def main_kernel(row_at, col_at, d_ref, *refs):
    bufs, (out_ref, sel, dcat) = refs[:-3], refs[-3:]
    rows, nnz = d_ref.shape[:2]
    width = nnz * BLK

    def one(i, carry):
        def clear(e, c):
            sel[pl.ds(pl.multiple_of(e * BLK, BLK), BLK), :] = jnp.zeros(
                (BLK, sel.shape[1]), BF16
            )
            return c

        lax.fori_loop(0, nnz, clear, 0)
        for e in range(nnz):
            dcat[:, e * BLK : (e + 1) * BLK] = d_ref[i, e]
        places = [(buf, j) for buf in bufs for j in range(buf.shape[0])]
        for q, (buf, j) in enumerate(places):
            e = row_at[i, q]

            @pl.when(e < nnz)
            def _():
                top = pl.multiple_of(e * BLK, BLK)

                def put(f, c):
                    g = col_at[i, q * nnz + f]
                    left = pl.multiple_of(g * BLK, BLK)
                    sel[pl.ds(top, BLK), pl.ds(left, BLK)] = buf[j, f]
                    return c

                lax.fori_loop(0, nnz, put, 0)

        def mult(n, c):
            at = pl.ds(pl.multiple_of(n * 256, 256), 256)
            out_ref[i, :, at] = jnp.dot(dcat[...], sel[:, at], preferred_element_type=F32)
            return c

        lax.fori_loop(0, width // 256, mult, 0)
        return carry

    lax.fori_loop(0, rows, one, 0)


def main_product(row_at, col_at, d, bufs):
    rows, nnz = d.shape[:2]
    return pl.pallas_call(
        main_kernel,
        out_shape=jax.ShapeDtypeStruct((rows, BLK, nnz * BLK), F32),
        in_specs=[SMEM, SMEM, VMEM] + [VMEM] * len(bufs),
        out_specs=VMEM,
        scratch_shapes=[
            pltpu.VMEM((nnz * BLK, (nnz + 1) * BLK), BF16),
            pltpu.VMEM((BLK, nnz * BLK), BF16),
        ],
        compiler_params=params(18),
        cost_estimate=cost(10, 10 << 20),
        name="hamiltonian",
    )(row_at, col_at, d, *bufs)


def final_kernel(at_ref, main_ref, d_ref, shift_ref, out_ref):
    rows, nnz = d_ref.shape[:2]
    for i in range(rows):
        for g in range(nnz):
            s = shift_ref[pl.ds(at_ref[i, g], 1), :]
            out_ref[i, g] = (
                main_ref[i, :, g * BLK : (g + 1) * BLK] + d_ref[i, g].astype(F32) * s
            ).astype(BF16)


def final(at, main, d, shift):
    return pl.pallas_call(
        final_kernel,
        out_shape=jax.ShapeDtypeStruct(d.shape, BF16),
        in_specs=[SMEM, VMEM, VMEM, VMEM],
        out_specs=VMEM,
        compiler_params=params(6),
        cost_estimate=cost(2, 4 << 20),
        name="final",
    )(at, main, d, shift)


ORDER = (0, 1, 3, 2)


def gather_hamiltonian(tiles, n_row):
    chips = n_row // 2
    assert chips == len(ORDER) and tiles.shape[0] == 2
    ahead = [(r, ((r // 2 + 1) % chips) * 2 + r % 2) for r in range(n_row)]
    behind = [(r, ((r // 2 - 1) % chips) * 2 + r % 2) for r in range(n_row)]
    one = lax.ppermute(tiles, "row", ahead)
    three = lax.ppermute(tiles, "row", behind)
    return one, three


def spread_hamiltonian(tiles, one, three, n_row):
    chips = n_row // 2
    ahead = [(r, ((r // 2 + 1) % chips) * 2 + r % 2) for r in range(n_row)]
    behind = [(r, ((r // 2 - 1) % chips) * 2 + r % 2) for r in range(n_row)]
    swap = [(r, r ^ 1) for r in range(n_row)]
    two_top = lax.ppermute(one[:1], "row", ahead)
    two_end = lax.ppermute(three[1:], "row", behind)
    same = [tiles, one, three, two_top, two_end]
    return same + [lax.ppermute(t, "row", swap) for t in same]


def positions(pattern, own_rows, n_row):
    me = lax.axis_index("row")
    chips = n_row // 2
    chip, core = me // 2, me % 2
    back = jnp.asarray(ORDER, jnp.int32)
    owner = (chip - back + chips) % chips * 2
    owner = jnp.concatenate([owner + core, owner + 1 - core])
    k = (owner[:, None] * own_rows + jnp.arange(own_rows, dtype=jnp.int32)).reshape(-1)
    own = lax.dynamic_slice_in_dim(pattern, me * own_rows, own_rows, 0)
    nnz = pattern.shape[1]
    local = own % (own_rows * n_row)
    index = jnp.arange(nnz, dtype=jnp.int32)
    row_at = jnp.min(
        jnp.where(local[:, None, :] == k[None, :, None], index, nnz), axis=2
    )
    rows = pattern[k]
    col_at = jnp.min(
        jnp.where(own[:, None, None, :] == rows[None, :, :, None], index, nnz), axis=3
    )
    shift_at = local // own_rows * 8 + local % own_rows
    return row_at, col_at.reshape(own_rows, -1), shift_at


def body(
    orbital_fragments,
    receiving_devices,
    fragment_grid_tile,
    outside_field_grid,
    density_matrix_tiles,
    energy_operator_tiles,
    tile_column_numbers,
):
    seg_dev = orbital_fragments.shape[0]
    n_orb = lax.axis_size("orb")
    n_row = lax.axis_size("row")
    devices = n_orb * n_row
    axes = ("orb", "row")

    def exchange(x, *block):
        pairs = x.reshape(devices, *block, LANES)
        got = lax.all_to_all(pairs, axes, split_axis=0, concat_axis=0, tiled=True)
        return got.reshape(-1, LANES)

    own_rows = density_matrix_tiles.shape[0]
    row_at, col_at, shift_at = positions(tile_column_numbers, own_rows, n_row)
    one, three = gather_hamiltonian(energy_operator_tiles, n_row)

    dest = receiving_devices.reshape(seg_dev // LANES, LANES)
    tile = fragment_grid_tile.reshape(seg_dev // LANES, LANES)
    me = (lax.axis_index("orb") * n_row + lax.axis_index("row")).reshape(1)
    outgoing, back = send_side(me, dest, tile, orbital_fragments, devices)
    arrived = exchange(outgoing, PAIR // 2, 2)
    bufs = spread_hamiltonian(energy_operator_tiles, one, three, n_row)
    main = main_product(row_at, col_at, density_matrix_tiles, bufs)

    arrived, main = lax.optimization_barrier((arrived, main))
    results, charge = owner_step(arrived, outside_field_grid)
    applied, shift = unpack(back, exchange(results, CAP), orbital_fragments, n_row)
    shift = lax.all_to_all(shift, "row", split_axis=0, concat_axis=0, tiled=True)
    product = final(shift_at, main, density_matrix_tiles, shift.reshape(n_row * 8, LANES))
    return (applied, charge, product)


def solution(mesh):
    return jax.shard_map(
        body,
        mesh=mesh,
        in_specs=(
            P(("orb", "row"), None),
            P(("orb", "row"), None),
            P(("orb", "row")),
            P(("orb", "row"), None),
            P(("orb", "row"), None, None, None),
            P(("orb", "row"), None, None, None),
            P("orb", None),
        ),
        out_specs=(
            P(("orb", "row"), None),
            P(("orb", "row"), None),
            P(("orb", "row"), None, None, None),
        ),
        check_vma=False,
    )
```
